32 devices in a mesh: px: 8 (over z, core), py: 4 (over y, x).
Axes of the slice: x: 2, y: 2, z: 4, core: 2. Of those that a mesh axis runs over, the one named last changes fastest.
Arguments:
- initial_heat_state: float32 [4, 1024, 1024], P(None, 'px', 'py'), may hold values from -6 to 7
- spreading_coefficient: float32 [4, 1024, 1024], P(None, 'px', 'py'), may hold values from 0.5 to 200000, as said below
Outputs:
- heat: float32 [4, 1024, 1024], P(None, 'px', 'py')
The draws below stay inside these ranges and needn't reach their ends.
Inputs may be any that keep to these rules, and one draw needn't show every extreme that they name: `spreading_coefficient`: positive in every cell.
All inputs are finite; a program needn't handle non-finite values.
Results may differ from the reference program's by a relative error of at most 0.0004.
Values sent between devices are 32-bit elements; how exact they have to be, the bound alone decides.
A program may use at most 64 MiB of HBM per device.

```python
import jax
import jax.numpy as jnp
from jax import lax

NX = 1024
NY = 1024
NZ = 4


def draw_spreading_coefficient(key, part):
    plane_key = jax.random.fold_in(key, 11)
    cell_key = jax.random.fold_in(key, 12)
    plane = 10.0 ** (5.0 * jax.random.uniform(plane_key, (NZ, 1, 1), jnp.float32))
    cell = 2.0 ** jax.random.uniform(cell_key, (NZ, NX, NY), jnp.float32, -1.0, 1.0)
    return (plane * cell).astype(jnp.float32)


def draw_initial_heat_state(key, part):
    rough_key = jax.random.fold_in(key, 21)
    along_x = jnp.sin(jnp.pi * (jnp.arange(NX).astype(jnp.float32) + 0.5) / NX)
    vertical_sweep_output = jnp.sin(jnp.pi * (jnp.arange(NY).astype(jnp.float32) + 0.5) / NY)
    smooth = along_x[None, :, None] * vertical_sweep_output[None, None, :]
    rough = jnp.clip(jax.random.normal(rough_key, (NZ, NX, NY), jnp.float32), -5.0, 5.0)
    result = rough + smooth
    return result.astype(jnp.float32)


def setup_inputs(seed: int = 0) -> dict:
    arg_keys = jax.random.split(jax.random.key(seed), 3)
    return {
        "initial_heat_state": draw_initial_heat_state(jax.random.fold_in(arg_keys[2], 71), 0),
        "spreading_coefficient": draw_spreading_coefficient(jax.random.fold_in(arg_keys[2], 71), 0),
    }


def thomas_algorithm(spreading_coefficient, source):
    lower = (-spreading_coefficient).at[0].set(0.0)
    upper = (-spreading_coefficient).at[-1].set(0.0)
    middle = 1.0 + 2.0 * spreading_coefficient
    zero = jnp.zeros(source.shape[1:], source.dtype)

    def forward(carry, inputs):
        ratio, value = carry
        low_now, mid_now, up_now, src_now = inputs
        divisor = mid_now - low_now * ratio
        ratio_new = up_now / divisor
        value_new = (src_now - low_now * value) / divisor
        return (ratio_new, value_new), (ratio_new, value_new)

    carried, (ratios, value_field) = lax.scan(forward, (zero, zero), (lower, middle, upper, source))

    def backward(later, inputs):
        ratio, value = inputs
        now = value - ratio * later
        return now, now

    carried, solved = lax.scan(backward, zero, (ratios, value_field), reverse=True)
    return solved


def reference(initial_heat_state, spreading_coefficient):
    padded_margin_grid = jnp.pad(initial_heat_state, 1)
    center = padded_margin_grid[1:-1, 1:-1, 1:-1]
    neighbours = padded_margin_grid[2:, 1:-1, 1:-1] + padded_margin_grid[:-2, 1:-1, 1:-1]
    neighbours = neighbours + padded_margin_grid[1:-1, 2:, 1:-1] + padded_margin_grid[1:-1, :-2, 1:-1]
    neighbours = neighbours + padded_margin_grid[1:-1, 1:-1, 2:] + padded_margin_grid[1:-1, 1:-1, :-2]
    source = center + 0.125 * (neighbours - 6.0 * center)
    after_x = jnp.moveaxis(thomas_algorithm(jnp.moveaxis(spreading_coefficient, 1, 0), jnp.moveaxis(source, 1, 0)), 0, 1)
    heat = jnp.moveaxis(thomas_algorithm(jnp.moveaxis(spreading_coefficient, 2, 0), jnp.moveaxis(after_x, 2, 0)), 0, 2)
    return heat
```

```python
import functools

import jax
import jax.numpy as jnp
from jax import lax
from jax.experimental import pallas as pl
from jax.experimental.pallas import tpu as pltpu
from jax.sharding import PartitionSpec as P

LANES = 128
BLOCKS = 8
MESH = pl.DeviceIdType.MESH


def combine(left, right):
    e_p, w_p, a_p = left
    e_q, w_q, a_q = right
    gap_p = e_p + w_p
    gap_q = e_q + a_q
    r_p = 1.0 - gap_p
    b_q = 1.0 - gap_q
    inv = 1.0 / (gap_p + r_p * gap_q)
    joined = (
        e_p * e_q * inv,
        w_q + e_q * ((w_p + r_p * a_q) * inv),
        a_p + e_p * ((a_q + b_q * w_p) * inv),
    )
    return joined, (inv, r_p, b_q, e_p, e_q)


def combine_rhs(node, left, right):
    inv, r_p, b_q, e_p, e_q = node
    u_p, a_p = left
    u_q, a_q = right
    p0 = (u_p + r_p * a_q) * inv
    q0 = (a_q + b_q * u_p) * inv
    return (u_q + e_q * p0, a_p + e_p * q0), (p0, q0)


def split(node, start, low, high):
    inv, r_p, b_q, e_p, e_q = node
    p = q = None
    if low is not None:
        from_low = e_p * inv * low
        p, q = from_low, b_q * from_low
    if high is not None:
        from_high = e_q * inv * high
        p = r_p * from_high if p is None else p + r_p * from_high
        q = from_high if q is None else q + from_high
    if start is not None:
        p = start[0] if p is None else start[0] + p
        q = start[1] if q is None else start[1] + q
    return p, q


def tree_coefficients(leaves):
    nodes = []
    while len(leaves) > 1:
        pairs = [combine(leaves[i], leaves[i + 1]) for i in range(0, len(leaves), 2)]
        leaves = [pair[0] for pair in pairs]
        nodes.append([pair[1] for pair in pairs])
    return leaves[0], nodes


def tree_up(nodes, leaves):
    starts = []
    for level in nodes:
        pairs = [
            combine_rhs(level[i], leaves[2 * i], leaves[2 * i + 1]) for i in range(len(level))
        ]
        leaves = [pair[0] for pair in pairs]
        starts.append([pair[1] for pair in pairs])
    return leaves[0], starts


def tree_down(nodes, starts, low, high):
    bounds = [(low, high)]
    for depth in range(len(nodes) - 1, -1, -1):
        below = []
        for i, (lo, hi) in enumerate(bounds):
            start = None if starts is None else starts[depth][i]
            p, q = split(nodes[depth][i], start, lo, hi)
            below += [(lo, q), (p, hi)]
        bounds = below
    zero = jnp.zeros_like(nodes[0][0][0])
    return [tuple(zero if x is None else x for x in pair) for pair in bounds]


def leaf_rows(turn_ref, values, count):
    turn_ref[0 : count * BLOCKS, :] = values.reshape(count * BLOCKS, LANES)
    return [turn_ref[pl.ds(b, count, stride=BLOCKS), :] for b in range(BLOCKS)]


def block_rows(turn_ref, rows, count):
    for b in range(BLOCKS):
        turn_ref[pl.ds(b, count, stride=BLOCKS), :] = rows[b]
    return turn_ref[0 : count * BLOCKS, :].reshape(count, BLOCKS, LANES)


def sweep_coefficients(m_ref, r_ref, e_ref, turn_refs, length):
    count = m_ref.shape[0]
    for g in range(length):
        m = m_ref[:, pl.ds(g, BLOCKS, stride=length), :]
        if g == 0:
            t = 1.0 + m
            r = 1.0 / (1.0 + t)
            e = r
            w = m * r
            a = w
        else:
            t = m + t * r
            r = 1.0 / (1.0 + t)
            w = (m + w) * r
            a = a + e * w
            e = e * r
        r_ref[g] = r
        e_ref[g] = e
    leaves = [leaf_rows(ref, value, count) for ref, value in zip(turn_refs, (e, w, a))]
    return tree_coefficients([tuple(leaf[b] for leaf in leaves) for b in range(BLOCKS)])


def responses(nodes, count, length, r_ref, e_ref, turns, store):
    one = jnp.ones((count, LANES), jnp.float32)
    bounds = tree_down(nodes, None, one, None)
    low_e = block_rows(turns[0], [b[0] for b in bounds], count)
    value_e = block_rows(turns[1], [b[1] for b in bounds], count)
    bounds = tree_down(nodes, None, None, one)
    low_w = block_rows(turns[2], [b[0] for b in bounds], count)
    value_w = block_rows(turns[3], [b[1] for b in bounds], count)
    for g in range(length - 1, -1, -1):
        e, r = e_ref[g], r_ref[g]
        value_e = e * low_e + r * value_e
        value_w = e * low_w + r * value_w
        store(g, value_e, value_w)


def own_solution(u, total, nodes, count, length, r_ref, e_ref, u_ref, turns, store):
    leaves = [leaf_rows(ref, value, count) for ref, value in zip(turns, (u, total))]
    _, starts = tree_up(nodes, list(zip(*leaves)))
    bounds = tree_down(nodes, starts, None, None)
    low = block_rows(turns[0], [b[0] for b in bounds], count)
    value = block_rows(turns[1], [b[1] for b in bounds], count)
    for g in range(length - 1, -1, -1):
        value = (u_ref[g] + e_ref[g] * low) + r_ref[g] * value
        store(g, value)


def interface_weights(gathered, me, n, side_ref, weight_ref):
    blocks = [tuple(gathered[i, c] for c in range(3)) for i in range(n)]
    zero = jnp.zeros_like(blocks[0][0])
    one = jnp.ones_like(zero)
    side_ref[0, 0], side_ref[1, 0] = zero, one
    side_ref[2, n], side_ref[3, n] = zero, one
    total = None
    factor, gap = zero, one
    up = []
    for j in range(n):
        e, w, a = blocks[j]
        t = e / (gap + factor * (e + a))
        up.append((t, factor))
        side_ref[4, j] = t
        total = blocks[j] if total is None else combine(total, blocks[j])[0]
        gap = total[0] + total[1]
        factor = 1.0 - gap
        side_ref[0, j + 1], side_ref[1, j + 1] = factor, gap
    total = None
    factor, gap = zero, one
    down = [None] * n
    for j in range(n - 1, -1, -1):
        e, w, a = blocks[j]
        s = e / ((e + w) + (1.0 - (e + w)) * gap)
        down[j] = (s, factor)
        side_ref[5, j] = s
        total = blocks[j] if total is None else combine(blocks[j], total)[0]
        gap = total[0] + total[2]
        factor = 1.0 - gap
        side_ref[2, j], side_ref[3, j] = factor, gap
    below, above = side_ref[0, me], side_ref[2, me + 1]
    at_low = 1.0 / (side_ref[1, me] + below * side_ref[3, me])
    at_high = 1.0 / (side_ref[1, me + 1] + side_ref[0, me + 1] * side_ref[3, me + 1])
    t, s = side_ref[4, me], side_ref[5, me]
    low_x, low_y = at_low, at_low * below * s
    high_x, high_y = at_high * above * t, at_high
    through = one
    for j in range(n - 1, -1, -1):
        inside = j < me
        keep = jnp.where(inside, through, 0.0)
        t_j, factor_j = up[j]
        other = keep * (t_j * factor_j)
        weight_ref[j, 0], weight_ref[j, 1] = low_x * keep, low_x * other
        weight_ref[j, 2], weight_ref[j, 3] = high_x * keep, high_x * other
        through = jnp.where(inside, through * t_j, through)
    through = one
    for j in range(n):
        inside = j > me
        keep = jnp.where(inside, through, 0.0)
        s_j, factor_j = down[j]
        other = keep * (s_j * factor_j)
        weight_ref[j, 0] += low_y * other
        weight_ref[j, 1] += low_y * keep
        weight_ref[j, 2] += high_y * other
        weight_ref[j, 3] += high_y * keep
        through = jnp.where(inside, through * s_j, through)
    weight_ref[me, 0] = low_y * above
    weight_ref[me, 1] = at_low * below
    weight_ref[me, 2] = at_high * above
    weight_ref[me, 3] = high_x * below


def outer_values(gathered, weight_ref, n):
    low, high = [], []
    for j in range(n):
        u, a = gathered[j, 0], gathered[j, 1]
        low.append(weight_ref[j, 0] * u + weight_ref[j, 1] * a)
        high.append(weight_ref[j, 2] * u + weight_ref[j, 3] * a)
    while len(low) > 1:
        low = [sum(low[i : i + 2]) for i in range(0, len(low), 2)]
        high = [sum(high[i : i + 2]) for i in range(0, len(high), 2)]
    return low[0], high[0]


def partner(me, d, n):
    if n & (n - 1):
        return lax.rem(me + d, n)
    at, b = me, 1
    while b < n:
        if d & b:
            at = at + b - 2 * b * lax.rem(lax.div(me, b), 2)
        b *= 2
    return at


def far_first(n):
    return sorted(range(1, n), key=lambda d: (-(d // 2), d % 2))


def kernel(
    nx,
    ny,
    h_hbm,
    k_hbm,
    out_ref,
    k_ref,
    h_ref,
    m_ref,
    mt_ref,
    rx_ref,
    ex_ref,
    ux_ref,
    fx_ref,
    vx_ref,
    px_ref,
    qx_ref,
    pm_ref,
    qm_ref,
    ry_ref,
    ey_ref,
    uy_ref,
    py_ref,
    qy_ref,
    pf_ref,
    qf_ref,
    mid_ref,
    midt_ref,
    turn0,
    turn1,
    turn2,
    turn3,
    hxs_ref,
    hxr_ref,
    hys_ref,
    hyr_ref,
    col_ref,
    cgx,
    rgx,
    cgy,
    rgy,
    sidex,
    sidey,
    weightx,
    weighty,
    in_sem,
    hs_sem,
    hr_sem,
    ps_sem,
    pr_sem,
):
    ix = lax.axis_index("px")
    iy = lax.axis_index("py")
    planes, rows, columns = h_hbm.shape
    tiles = columns // LANES
    count = tiles * planes
    lx = rows // BLOCKS
    ly = columns // BLOCKS
    turns = (turn0, turn1, turn2, turn3)
    f32 = jnp.float32

    def stage(source, target, j, number):
        return pltpu.make_async_copy(
            source.at[:, :, pl.ds(j * LANES, LANES)],
            target.at[pl.ds(j * planes, planes)],
            in_sem.at[number],
        )

    stage_k = [stage(k_hbm, k_ref, j, j) for j in range(tiles)]
    stage_h = [stage(h_hbm, h_ref, j, tiles + j) for j in range(tiles)]
    for copy in stage_h:
        copy.start()

    barrier = pltpu.get_barrier_semaphore()
    for d in range(1, nx):
        pl.semaphore_signal(barrier, inc=1, device_id=(partner(ix, d, nx), iy), device_id_type=MESH)
    for d in range(1, ny):
        pl.semaphore_signal(barrier, inc=1, device_id=(ix, partner(iy, d, ny)), device_id_type=MESH)

    for copy in stage_k:
        copy.start()

    def exchange(ref, number, me, n, along_x):
        copies = []
        for d in far_first(n) if along_x else range(n - 1, 0, -1):
            to = partner(me, d, n)
            copies.append(
                pltpu.make_async_remote_copy(
                    src_ref=ref.at[me],
                    dst_ref=ref.at[me],
                    send_sem=ps_sem.at[number],
                    recv_sem=pr_sem.at[number],
                    device_id=(to, iy) if along_x else (ix, to),
                    device_id_type=MESH,
                )
            )
        for copy in copies:
            copy.start()
        others = ref.at[pl.ds(0, n - 1)]
        return (
            pltpu.make_async_copy(others, others, ps_sem.at[number]),
            pltpu.make_async_copy(others, others, pr_sem.at[number]),
        )

    @pl.when(ix == 0)
    def _():
        hxr_ref[0] = jnp.zeros_like(hxr_ref[0])

    @pl.when(ix == nx - 1)
    def _():
        hxr_ref[1] = jnp.zeros_like(hxr_ref[1])

    low_side = pl.ds(0, planes)
    high_side = pl.ds(planes, planes)

    @pl.when(iy == 0)
    def _():
        hyr_ref[low_side] = jnp.zeros((planes, LANES), f32)

    @pl.when(iy == ny - 1)
    def _():
        hyr_ref[high_side] = jnp.zeros((planes, LANES), f32)

    def halo(source, target, number, device):
        return pltpu.make_async_remote_copy(
            src_ref=source,
            dst_ref=target,
            send_sem=hs_sem.at[number],
            recv_sem=hr_sem.at[number],
            device_id=device,
            device_id_type=MESH,
        )

    x_down = halo(hxs_ref.at[0], hxr_ref.at[1], 0, (lax.rem(ix + nx - 1, nx), iy))
    x_up = halo(hxs_ref.at[1], hxr_ref.at[0], 1, (lax.rem(ix + 1, nx), iy))
    y_down = halo(
        hys_ref.at[low_side], hyr_ref.at[high_side], 2, (ix, lax.rem(iy + ny - 1, ny))
    )
    y_up = halo(hys_ref.at[high_side], hyr_ref.at[low_side], 3, (ix, lax.rem(iy + 1, ny)))
    routes = (
        (y_down, iy > 0, iy < ny - 1),
        (y_up, iy < ny - 1, iy > 0),
        (x_down, ix > 0, ix < nx - 1),
        (x_up, ix < nx - 1, ix > 0),
    )

    lane = lax.broadcasted_iota(jnp.int32, (rows, LANES), 1)

    def edge_columns(ref):
        packed = jnp.zeros((rows, LANES), f32)
        for p in range(planes):
            low = ref[p]
            high = ref[(tiles - 1) * planes + p]
            packed = jnp.where(lane == p, low if p == 0 else pltpu.roll(low, p, 1), packed)
            packed = jnp.where(lane == planes + p, pltpu.roll(high, planes + p + 1, 1), packed)
        return packed.T[0 : 2 * planes]

    for copy in stage_h:
        copy.wait()
    hxs_ref[0] = h_ref[:, 0, :]
    hxs_ref[1] = h_ref[:, rows - 1, :]
    hys_ref[...] = edge_columns(h_ref)

    pl.semaphore_wait(barrier, nx + ny - 2)
    for copy, sends, _ in routes:
        pl.when(sends)(copy.start)

    for j in range(tiles):
        part = pl.ds(j * planes, planes)
        stage_k[j].wait()
        m_ref[part] = 1.0 / k_ref[part]
    joined, nodes_x = sweep_coefficients(m_ref, rx_ref, ex_ref, turns, lx)
    for c in range(3):
        cgx[ix, c] = joined[c]
    sent_cx, got_cx = exchange(cgx, 0, ix, nx, True)
    top_e, top_w, top_a = joined

    for p in range(planes):
        for j in range(tiles):
            mt_ref[p, pl.ds(j * LANES, LANES), :] = m_ref[j * planes + p].T
    joined, nodes_y = sweep_coefficients(mt_ref, ry_ref, ey_ref, turns, ly)
    for c in range(3):
        cgy[iy, c] = joined[c]
    sent_cy, got_cy = exchange(cgy, 1, iy, ny, False)

    def store_responses_x(g, e, w):
        px_ref[g], qx_ref[g] = e, w
        at = pl.ds(g, BLOCKS, stride=lx)
        m = 0.125 * m_ref[:, at, :]
        pm_ref[:, at, :] = m * e
        qm_ref[:, at, :] = m * w

    responses(nodes_x, count, lx, rx_ref, ex_ref, turns, store_responses_x)
    edge_p, edge_q = edge_columns(pm_ref), edge_columns(qm_ref)

    def field(g):
        return h_ref[:, pl.ds(g, BLOCKS, stride=lx), :]

    shape = (count, BLOCKS, LANES)
    sub = lax.broadcasted_iota(jnp.int32, shape, 1)
    lane1 = lax.broadcasted_iota(jnp.int32, (BLOCKS, LANES), 1)
    none = jnp.zeros((BLOCKS, LANES), f32)
    now = field(0)
    before = jnp.where(sub == 0, 0.0, pltpu.roll(field(lx - 1), 1, 1))
    beyond = jnp.where(sub == BLOCKS - 1, 0.0, pltpu.roll(now, BLOCKS - 1, 1))
    sum_u = sum_a = None
    for g in range(lx):
        after = field(g + 1) if g + 1 < lx else beyond
        to_right = pltpu.roll(now, 1, 2)
        to_left = pltpu.roll(now, LANES - 1, 2)
        around = []
        for j in range(tiles):
            for p in range(planes):
                i = j * planes + p
                low = none if j == 0 else to_right[i - planes]
                high = none if j == tiles - 1 else to_left[i + planes]
                left = jnp.where(lane1 == 0, low, to_right[i])
                right = jnp.where(lane1 == LANES - 1, high, to_left[i])
                under = now[i - 1] if p > 0 else none
                over = now[i + 1] if p < planes - 1 else none
                around.append((over + under) + (left + right))
        around = jnp.stack(around) + (after + before)
        source = now + 0.125 * (around - 6.0 * now)
        f = source * m_ref[:, pl.ds(g, BLOCKS, stride=lx), :]
        fx_ref[g] = f
        sum_u = f * qx_ref[g] if g == 0 else sum_u + f * qx_ref[g]
        sum_a = f * px_ref[g] if g == 0 else sum_a + f * px_ref[g]
        before, now = now, after
    sum_u, sum_a = jnp.sum(sum_u, axis=1), jnp.sum(sum_a, axis=1)
    m_first, m_last = 0.125 * m_ref[:, 0, :], 0.125 * m_ref[:, rows - 1, :]
    factor_w = 1.0 - (top_e + top_w)
    factor_a = 1.0 - (top_e + top_a)

    at_row = lax.broadcasted_iota(jnp.int32, (count, LANES), 0)
    at_lane = lax.broadcasted_iota(jnp.int32, (count, LANES), 1)
    on_edge = ((at_row < planes) & (at_lane == 0)) | (
        (at_row >= count - planes) & (at_lane == LANES - 1)
    )

    def spread_edge(value):
        value = jnp.sum(value, axis=1, keepdims=True)
        if count > 2 * planes:
            gap = jnp.zeros((count - 2 * planes, 1), f32)
            value = jnp.concatenate([value[0:planes], gap, value[planes:]], axis=0)
        return jnp.where(on_edge, value, 0.0)

    for copy, _, receives in routes:
        pl.when(receives)(copy.wait_recv)
    sides = hyr_ref[...]
    shift_low, shift_high = m_first * hxr_ref[0], m_last * hxr_ref[1]
    rgx[ix, 0] = (sum_u + spread_edge(sides * edge_q)) + (
        top_e * shift_low + factor_w * shift_high
    )
    rgx[ix, 1] = (sum_a + spread_edge(sides * edge_p)) + (
        factor_a * shift_low + top_e * shift_high
    )
    sent_rx, got_rx = exchange(rgx, 2, ix, nx, True)

    spread = jnp.concatenate([sides, jnp.zeros((LANES - 2 * planes, LANES), f32)], axis=0)
    col_ref[...] = spread.T
    u = total = None
    for g in range(lx):
        at = pl.ds(g, BLOCKS, stride=lx)
        column = 0.125 * col_ref[at, :]
        f = fx_ref[g]
        parts = [f[i] for i in range(count)]
        for p in range(planes):
            low = column if p == 0 else pltpu.roll(column, LANES - p, 1)
            high = pltpu.roll(column, LANES - 1 - planes - p, 1)
            i = p
            parts[i] = parts[i] + jnp.where(lane1 == 0, low, 0.0) * m_ref[i, at, :]
            i = (tiles - 1) * planes + p
            parts[i] = parts[i] + jnp.where(lane1 == LANES - 1, high, 0.0) * m_ref[i, at, :]
        f = jnp.stack(parts)
        u = (f if g == 0 else f + u) * rx_ref[g]
        total = u if g == 0 else total + ex_ref[g - 1] * u
        ux_ref[g] = u

    def store_x(g, value):
        vx_ref[g] = value

    own_solution(u, total, nodes_x, count, lx, rx_ref, ex_ref, ux_ref, turns, store_x)

    def store_responses_y(g, e, w):
        at = pl.ds(g, BLOCKS, stride=ly)
        py_ref[:, at, :] = e
        qy_ref[:, at, :] = w

    responses(nodes_y, planes, ly, ry_ref, ey_ref, turns, store_responses_y)
    for p in range(planes):
        for j in range(tiles):
            at = pl.ds(j * LANES, LANES)
            m = mt_ref[p, at, :]
            pm_ref[j * planes + p] = (m * py_ref[p, at, :]).T
            qm_ref[j * planes + p] = (m * qy_ref[p, at, :]).T
    for g in range(lx):
        at = pl.ds(g, BLOCKS, stride=lx)
        pf_ref[g] = pm_ref[:, at, :]
        qf_ref[g] = qm_ref[:, at, :]
    got_cx.wait()
    interface_weights(cgx, ix, nx, sidex, weightx)

    got_rx.wait()
    low, high = outer_values(rgx, weightx, nx)
    low = jnp.broadcast_to((low + shift_low)[:, None, :], shape)
    high = jnp.broadcast_to((high + shift_high)[:, None, :], shape)
    lane_of = lax.broadcasted_iota(jnp.int32, (planes, BLOCKS, LANES), 2)
    block_of = lax.broadcasted_iota(jnp.int32, (planes, BLOCKS, LANES), 1)
    sum_u = jnp.zeros((planes, BLOCKS, LANES), f32)
    sum_a = sum_u
    for g in range(lx):
        v = (vx_ref[g] + px_ref[g] * low) + qx_ref[g] * high
        mid_ref[:, pl.ds(g, BLOCKS, stride=lx), :] = v
        of_u = jnp.sum((v * qf_ref[g]).reshape(tiles, planes, BLOCKS, LANES), axis=0)
        of_a = jnp.sum((v * pf_ref[g]).reshape(tiles, planes, BLOCKS, LANES), axis=0)
        here = lax.rem(lane_of, lx) == g
        sum_u = jnp.where(here, jnp.sum(of_u, axis=2, keepdims=True), sum_u)
        sum_a = jnp.where(here, jnp.sum(of_a, axis=2, keepdims=True), sum_a)
    diagonal = lax.div(lane_of, lx) == block_of
    rgy[iy, 0] = jnp.sum(jnp.where(diagonal, sum_u, 0.0), axis=1)
    rgy[iy, 1] = jnp.sum(jnp.where(diagonal, sum_a, 0.0), axis=1)
    sent_ry, got_ry = exchange(rgy, 3, iy, ny, False)

    for p in range(planes):
        for j in range(tiles):
            midt_ref[p, pl.ds(j * LANES, LANES), :] = mid_ref[j * planes + p].T
    u = total = None
    for g in range(ly):
        at = pl.ds(g, BLOCKS, stride=ly)
        f = midt_ref[:, at, :] * mt_ref[:, at, :]
        u = (f if g == 0 else f + u) * ry_ref[g]
        total = u if g == 0 else total + ey_ref[g - 1] * u
        uy_ref[g] = u

    def store_y(g, value):
        midt_ref[:, pl.ds(g, BLOCKS, stride=ly), :] = value

    own_solution(u, total, nodes_y, planes, ly, ry_ref, ey_ref, uy_ref, turns, store_y)
    got_cy.wait()
    interface_weights(cgy, iy, ny, sidey, weighty)
    for copy, sends, _ in routes:
        pl.when(sends)(copy.wait_send)
    for copy in (sent_cx, sent_cy, sent_rx):
        copy.wait()

    got_ry.wait()
    low, high = outer_values(rgy, weighty, ny)
    for p in range(planes):
        for j in range(tiles):
            at = pl.ds(j * LANES, LANES)
            value = midt_ref[p, at, :] + py_ref[p, at, :] * low[p : p + 1]
            value = value + qy_ref[p, at, :] * high[p : p + 1]
            out_ref[p, :, at] = value.T
    sent_ry.wait()


def on_device(nx, ny, initial_heat_state, spreading_coefficient):
    planes, rows, columns = initial_heat_state.shape
    count = planes * (columns // LANES)
    lx = rows // BLOCKS
    ly = columns // BLOCKS

    def vmem(*shape):
        return pltpu.VMEM(shape, jnp.float32)

    def dma(number):
        return pltpu.SemaphoreType.DMA((number,))

    natural = vmem(count, rows, LANES)
    turned = vmem(planes, columns, LANES)
    steps_x = vmem(lx, count, BLOCKS, LANES)
    steps_y = vmem(ly, planes, BLOCKS, LANES)
    return pl.pallas_call(
        functools.partial(kernel, nx, ny),
        out_shape=jax.ShapeDtypeStruct((planes, rows, columns), jnp.float32),
        in_specs=[pl.BlockSpec(memory_space=pltpu.HBM)] * 2,
        out_specs=pl.BlockSpec(memory_space=pltpu.VMEM),
        scratch_shapes=[
            natural,
            natural,
            natural,
            turned,
            steps_x,
            steps_x,
            steps_x,
            steps_x,
            steps_x,
            steps_x,
            steps_x,
            natural,
            natural,
            steps_y,
            steps_y,
            steps_y,
            turned,
            turned,
            steps_x,
            steps_x,
            natural,
            turned,
            vmem(count * BLOCKS, LANES),
            vmem(count * BLOCKS, LANES),
            vmem(count * BLOCKS, LANES),
            vmem(count * BLOCKS, LANES),
            vmem(2, count, LANES),
            vmem(2, count, LANES),
            vmem(2 * planes, LANES),
            vmem(2 * planes, LANES),
            vmem(rows, LANES),
            vmem(nx, 3, count, LANES),
            vmem(nx, 2, count, LANES),
            vmem(ny, 3, planes, LANES),
            vmem(ny, 2, planes, LANES),
            vmem(6, nx + 1, count, LANES),
            vmem(6, ny + 1, planes, LANES),
            vmem(nx, 4, count, LANES),
            vmem(ny, 4, planes, LANES),
            dma(2 * (columns // LANES)),
            dma(4),
            dma(4),
            dma(4),
            dma(4),
        ],
        compiler_params=pltpu.CompilerParams(
            collective_id=0, has_side_effects=True, vmem_limit_bytes=32 << 20
        ),
    )(
        pltpu.with_memory_space_constraint(initial_heat_state, pltpu.HBM),
        pltpu.with_memory_space_constraint(spreading_coefficient, pltpu.HBM),
    )


def solution(mesh):
    return jax.shard_map(
        functools.partial(on_device, mesh.shape["px"], mesh.shape["py"]),
        mesh=mesh,
        in_specs=(P(None, "px", "py"), P(None, "px", "py")),
        out_specs=P(None, "px", "py"),
        check_vma=False,
    )
```

```python
import functools

import jax
import jax.numpy as jnp
from jax import lax
from jax.experimental import pallas as pl
from jax.experimental.pallas import tpu as pltpu
from jax.sharding import PartitionSpec as P

LANES = 128
BLOCKS = 8
MESH = pl.DeviceIdType.MESH


def combine(left, right):
    e_p, w_p, a_p = left
    e_q, w_q, a_q = right
    gap_p = e_p + w_p
    gap_q = e_q + a_q
    r_p = 1.0 - gap_p
    b_q = 1.0 - gap_q
    inv = 1.0 / (gap_p + r_p * gap_q)
    joined = (
        e_p * e_q * inv,
        w_q + e_q * ((w_p + r_p * a_q) * inv),
        a_p + e_p * ((a_q + b_q * w_p) * inv),
    )
    return joined, (inv, r_p, b_q, e_p, e_q)


def combine_rhs(node, left, right):
    inv, r_p, b_q, e_p, e_q = node
    u_p, a_p = left
    u_q, a_q = right
    p0 = (u_p + r_p * a_q) * inv
    q0 = (a_q + b_q * u_p) * inv
    return (u_q + e_q * p0, a_p + e_p * q0), (p0, q0)


def split(node, start, low, high):
    inv, r_p, b_q, e_p, e_q = node
    p = q = None
    if low is not None:
        from_low = e_p * inv * low
        p, q = from_low, b_q * from_low
    if high is not None:
        from_high = e_q * inv * high
        p = r_p * from_high if p is None else p + r_p * from_high
        q = from_high if q is None else q + from_high
    if start is not None:
        p = start[0] if p is None else start[0] + p
        q = start[1] if q is None else start[1] + q
    return p, q


def tree_coefficients(leaves):
    nodes = []
    while len(leaves) > 1:
        pairs = [combine(leaves[i], leaves[i + 1]) for i in range(0, len(leaves), 2)]
        leaves = [pair[0] for pair in pairs]
        nodes.append([pair[1] for pair in pairs])
    return leaves[0], nodes


def tree_up(nodes, leaves):
    starts = []
    for level in nodes:
        pairs = [
            combine_rhs(level[i], leaves[2 * i], leaves[2 * i + 1]) for i in range(len(level))
        ]
        leaves = [pair[0] for pair in pairs]
        starts.append([pair[1] for pair in pairs])
    return leaves[0], starts


def tree_down(nodes, starts, low, high):
    bounds = [(low, high)]
    for depth in range(len(nodes) - 1, -1, -1):
        below = []
        for i, (lo, hi) in enumerate(bounds):
            start = None if starts is None else starts[depth][i]
            p, q = split(nodes[depth][i], start, lo, hi)
            below += [(lo, q), (p, hi)]
        bounds = below
    zero = jnp.zeros_like(nodes[0][0][0])
    return [tuple(zero if x is None else x for x in pair) for pair in bounds]


def leaf_rows(turn_ref, values, count):
    turn_ref[0 : count * BLOCKS, :] = values.reshape(count * BLOCKS, LANES)
    return [turn_ref[pl.ds(b, count, stride=BLOCKS), :] for b in range(BLOCKS)]


def block_rows(turn_ref, rows, count):
    for b in range(BLOCKS):
        turn_ref[pl.ds(b, count, stride=BLOCKS), :] = rows[b]
    return turn_ref[0 : count * BLOCKS, :].reshape(count, BLOCKS, LANES)


def sweep_coefficients(m_ref, r_ref, e_ref, turn_refs, length):
    count = m_ref.shape[0]
    for g in range(length):
        m = m_ref[:, pl.ds(g, BLOCKS, stride=length), :]
        if g == 0:
            t = 1.0 + m
            r = 1.0 / (1.0 + t)
            e = r
            w = m * r
            a = w
        else:
            t = m + t * r
            r = 1.0 / (1.0 + t)
            w = (m + w) * r
            a = a + e * w
            e = e * r
        r_ref[g] = r
        e_ref[g] = e
    leaves = [leaf_rows(ref, value, count) for ref, value in zip(turn_refs, (e, w, a))]
    return tree_coefficients([tuple(leaf[b] for leaf in leaves) for b in range(BLOCKS)])


def responses(nodes, count, length, r_ref, e_ref, turns, store):
    one = jnp.ones((count, LANES), jnp.float32)
    bounds = tree_down(nodes, None, one, None)
    low_e = block_rows(turns[0], [b[0] for b in bounds], count)
    value_e = block_rows(turns[1], [b[1] for b in bounds], count)
    bounds = tree_down(nodes, None, None, one)
    low_w = block_rows(turns[2], [b[0] for b in bounds], count)
    value_w = block_rows(turns[3], [b[1] for b in bounds], count)
    for g in range(length - 1, -1, -1):
        e, r = e_ref[g], r_ref[g]
        value_e = e * low_e + r * value_e
        value_w = e * low_w + r * value_w
        store(g, value_e, value_w)


def own_solution(u, total, nodes, count, length, r_ref, e_ref, u_ref, turns, store):
    leaves = [leaf_rows(ref, value, count) for ref, value in zip(turns, (u, total))]
    _, starts = tree_up(nodes, list(zip(*leaves)))
    bounds = tree_down(nodes, starts, None, None)
    low = block_rows(turns[0], [b[0] for b in bounds], count)
    value = block_rows(turns[1], [b[1] for b in bounds], count)
    for g in range(length - 1, -1, -1):
        value = (u_ref[g] + e_ref[g] * low) + r_ref[g] * value
        store(g, value)


def interface_weights(gathered, me, n, side_ref, weight_ref):
    blocks = [tuple(gathered[i, c] for c in range(3)) for i in range(n)]
    zero = jnp.zeros_like(blocks[0][0])
    one = jnp.ones_like(zero)
    side_ref[0, 0], side_ref[1, 0] = zero, one
    side_ref[2, n], side_ref[3, n] = zero, one
    total = None
    factor, gap = zero, one
    up = []
    for j in range(n):
        e, w, a = blocks[j]
        t = e / (gap + factor * (e + a))
        up.append((t, factor))
        side_ref[4, j] = t
        total = blocks[j] if total is None else combine(total, blocks[j])[0]
        gap = total[0] + total[1]
        factor = 1.0 - gap
        side_ref[0, j + 1], side_ref[1, j + 1] = factor, gap
    total = None
    factor, gap = zero, one
    down = [None] * n
    for j in range(n - 1, -1, -1):
        e, w, a = blocks[j]
        s = e / ((e + w) + (1.0 - (e + w)) * gap)
        down[j] = (s, factor)
        side_ref[5, j] = s
        total = blocks[j] if total is None else combine(blocks[j], total)[0]
        gap = total[0] + total[2]
        factor = 1.0 - gap
        side_ref[2, j], side_ref[3, j] = factor, gap
    below, above = side_ref[0, me], side_ref[2, me + 1]
    at_low = 1.0 / (side_ref[1, me] + below * side_ref[3, me])
    at_high = 1.0 / (side_ref[1, me + 1] + side_ref[0, me + 1] * side_ref[3, me + 1])
    t, s = side_ref[4, me], side_ref[5, me]
    low_x, low_y = at_low, at_low * below * s
    high_x, high_y = at_high * above * t, at_high
    through = one
    for j in range(n - 1, -1, -1):
        inside = j < me
        keep = jnp.where(inside, through, 0.0)
        t_j, factor_j = up[j]
        other = keep * (t_j * factor_j)
        weight_ref[j, 0], weight_ref[j, 1] = low_x * keep, low_x * other
        weight_ref[j, 2], weight_ref[j, 3] = high_x * keep, high_x * other
        through = jnp.where(inside, through * t_j, through)
    through = one
    for j in range(n):
        inside = j > me
        keep = jnp.where(inside, through, 0.0)
        s_j, factor_j = down[j]
        other = keep * (s_j * factor_j)
        weight_ref[j, 0] += low_y * other
        weight_ref[j, 1] += low_y * keep
        weight_ref[j, 2] += high_y * other
        weight_ref[j, 3] += high_y * keep
        through = jnp.where(inside, through * s_j, through)
    weight_ref[me, 0] = low_y * above
    weight_ref[me, 1] = at_low * below
    weight_ref[me, 2] = at_high * above
    weight_ref[me, 3] = high_x * below


def outer_values(gathered, weight_ref, n):
    low, high = [], []
    for j in range(n):
        u, a = gathered[j, 0], gathered[j, 1]
        low.append(weight_ref[j, 0] * u + weight_ref[j, 1] * a)
        high.append(weight_ref[j, 2] * u + weight_ref[j, 3] * a)
    while len(low) > 1:
        low = [sum(low[i : i + 2]) for i in range(0, len(low), 2)]
        high = [sum(high[i : i + 2]) for i in range(0, len(high), 2)]
    return low[0], high[0]


def partner(me, d, n):
    if n & (n - 1):
        return lax.rem(me + d, n)
    at, b = me, 1
    while b < n:
        if d & b:
            at = at + b - 2 * b * lax.rem(lax.div(me, b), 2)
        b *= 2
    return at


def far_first(n):
    return sorted(range(1, n), key=lambda d: (-(d // 2), d % 2))


def kernel(
    nx,
    ny,
    h_hbm,
    k_hbm,
    out_ref,
    k_ref,
    h_ref,
    m_ref,
    mt_ref,
    rx_ref,
    ex_ref,
    ux_ref,
    fx_ref,
    vx_ref,
    px_ref,
    qx_ref,
    pm_ref,
    qm_ref,
    ry_ref,
    ey_ref,
    uy_ref,
    py_ref,
    qy_ref,
    pf_ref,
    qf_ref,
    mid_ref,
    midt_ref,
    turn0,
    turn1,
    turn2,
    turn3,
    hxs_ref,
    hxr_ref,
    hys_ref,
    hyr_ref,
    col_ref,
    cgx,
    rgx,
    cgy,
    rgy,
    sidex,
    sidey,
    weightx,
    weighty,
    in_sem,
    hs_sem,
    hr_sem,
    ps_sem,
    pr_sem,
):
    ix = lax.axis_index("px")
    iy = lax.axis_index("py")
    planes, rows, columns = h_hbm.shape
    tiles = columns // LANES
    count = tiles * planes
    lx = rows // BLOCKS
    ly = columns // BLOCKS
    turns = (turn0, turn1, turn2, turn3)
    f32 = jnp.float32

    def stage(source, target, number):
        for j in range(tiles):
            pltpu.make_async_copy(
                source.at[:, :, pl.ds(j * LANES, LANES)],
                target.at[pl.ds(j * planes, planes)],
                in_sem.at[number],
            ).start()
        return pltpu.make_async_copy(target, target, in_sem.at[number])

    barrier = pltpu.get_barrier_semaphore()
    for d in far_first(nx):
        pl.semaphore_signal(barrier, inc=1, device_id=(partner(ix, d, nx), iy), device_id_type=MESH)
    for d in range(ny - 1, 0, -1):
        pl.semaphore_signal(barrier, inc=1, device_id=(ix, partner(iy, d, ny)), device_id_type=MESH)

    staged_h = stage(h_hbm, h_ref, 0)
    staged_k = stage(k_hbm, k_ref, 1)

    sent = []

    def exchange(ref, number, me, n, along_x):
        copies = []
        for d in far_first(n) if along_x else range(n - 1, 0, -1):
            to = partner(me, d, n)
            copies.append(
                pltpu.make_async_remote_copy(
                    src_ref=ref.at[me],
                    dst_ref=ref.at[me],
                    send_sem=ps_sem.at[number],
                    recv_sem=pr_sem.at[number],
                    device_id=(to, iy) if along_x else (ix, to),
                    device_id_type=MESH,
                )
            )
        for copy in copies:
            copy.start()
        others = ref.at[pl.ds(0, n - 1)]
        sent.append(pltpu.make_async_copy(others, others, ps_sem.at[number]))
        return pltpu.make_async_copy(others, others, pr_sem.at[number])

    @pl.when(ix == 0)
    def _():
        hxr_ref[0] = jnp.zeros_like(hxr_ref[0])

    @pl.when(ix == nx - 1)
    def _():
        hxr_ref[1] = jnp.zeros_like(hxr_ref[1])

    low_side = pl.ds(0, planes)
    high_side = pl.ds(planes, planes)

    @pl.when(iy == 0)
    def _():
        hyr_ref[low_side] = jnp.zeros((planes, LANES), f32)

    @pl.when(iy == ny - 1)
    def _():
        hyr_ref[high_side] = jnp.zeros((planes, LANES), f32)

    def halo(source, target, number, device):
        return pltpu.make_async_remote_copy(
            src_ref=source,
            dst_ref=target,
            send_sem=hs_sem.at[number],
            recv_sem=hr_sem.at[number],
            device_id=device,
            device_id_type=MESH,
        )

    x_down = halo(hxs_ref.at[0], hxr_ref.at[1], 0, (lax.rem(ix + nx - 1, nx), iy))
    x_up = halo(hxs_ref.at[1], hxr_ref.at[0], 0, (lax.rem(ix + 1, nx), iy))
    y_down = halo(
        hys_ref.at[low_side], hyr_ref.at[high_side], 1, (ix, lax.rem(iy + ny - 1, ny))
    )
    y_up = halo(hys_ref.at[high_side], hyr_ref.at[low_side], 1, (ix, lax.rem(iy + 1, ny)))
    routes = (
        (y_down, iy > 0),
        (y_up, iy < ny - 1),
        (x_down, ix > 0),
        (x_up, ix < nx - 1),
    )

    def wait_halos(sem, x_ref, y_ref):
        inner_x = (ix > 0) & (ix < nx - 1)
        inner_y = (iy > 0) & (iy < ny - 1)
        for ref, part, number, inner in (
            (x_ref, x_ref.at[0], 0, inner_x),
            (y_ref, y_ref.at[low_side], 1, inner_y),
        ):
            pl.when(inner)(pltpu.make_async_copy(ref, ref, sem.at[number]).wait)
            pl.when(jnp.logical_not(inner))(pltpu.make_async_copy(part, part, sem.at[number]).wait)

    lane = lax.broadcasted_iota(jnp.int32, (rows, LANES), 1)

    def edge_columns(ref):
        packed = jnp.zeros((rows, LANES), f32)
        for p in range(planes):
            low = ref[p]
            high = ref[(tiles - 1) * planes + p]
            packed = jnp.where(lane == p, low if p == 0 else pltpu.roll(low, p, 1), packed)
            packed = jnp.where(lane == planes + p, pltpu.roll(high, planes + p + 1, 1), packed)
        return packed.T[0 : 2 * planes]

    staged_h.wait()
    hxs_ref[0] = h_ref[:, 0, :]
    hxs_ref[1] = h_ref[:, rows - 1, :]
    hys_ref[...] = edge_columns(h_ref)

    pl.semaphore_wait(barrier, nx + ny - 2)
    for copy, sends in routes:
        pl.when(sends)(copy.start)

    staged_k.wait()
    m_ref[...] = 1.0 / k_ref[...]
    joined, nodes_x = sweep_coefficients(m_ref, rx_ref, ex_ref, turns, lx)
    for c in range(3):
        cgx[ix, c] = joined[c]
    got_cx = exchange(cgx, 0, ix, nx, True)
    top_e, top_w, top_a = joined

    def store_responses_x(g, e, w):
        px_ref[g], qx_ref[g] = e, w
        at = pl.ds(g, BLOCKS, stride=lx)
        m = 0.125 * m_ref[:, at, :]
        pm_ref[:, at, :] = m * e
        qm_ref[:, at, :] = m * w

    responses(nodes_x, count, lx, rx_ref, ex_ref, turns, store_responses_x)
    edge_p, edge_q = edge_columns(pm_ref), edge_columns(qm_ref)

    def field(g):
        return h_ref[:, pl.ds(g, BLOCKS, stride=lx), :]

    shape = (count, BLOCKS, LANES)
    sub = lax.broadcasted_iota(jnp.int32, shape, 1)
    lane1 = lax.broadcasted_iota(jnp.int32, (BLOCKS, LANES), 1)
    none = jnp.zeros((BLOCKS, LANES), f32)
    now = field(0)
    before = jnp.where(sub == 0, 0.0, pltpu.roll(field(lx - 1), 1, 1))
    beyond = jnp.where(sub == BLOCKS - 1, 0.0, pltpu.roll(now, BLOCKS - 1, 1))
    sum_u = sum_a = None
    for g in range(lx):
        after = field(g + 1) if g + 1 < lx else beyond
        to_right = pltpu.roll(now, 1, 2)
        to_left = pltpu.roll(now, LANES - 1, 2)
        around = []
        for j in range(tiles):
            for p in range(planes):
                i = j * planes + p
                low = none if j == 0 else to_right[i - planes]
                high = none if j == tiles - 1 else to_left[i + planes]
                left = jnp.where(lane1 == 0, low, to_right[i])
                right = jnp.where(lane1 == LANES - 1, high, to_left[i])
                under = now[i - 1] if p > 0 else none
                over = now[i + 1] if p < planes - 1 else none
                around.append((over + under) + (left + right))
        around = jnp.stack(around) + (after + before)
        source = now + 0.125 * (around - 6.0 * now)
        f = source * m_ref[:, pl.ds(g, BLOCKS, stride=lx), :]
        fx_ref[g] = f
        sum_u = f * qx_ref[g] if g == 0 else sum_u + f * qx_ref[g]
        sum_a = f * px_ref[g] if g == 0 else sum_a + f * px_ref[g]
        before, now = now, after
    sum_u, sum_a = jnp.sum(sum_u, axis=1), jnp.sum(sum_a, axis=1)
    m_first, m_last = 0.125 * m_ref[:, 0, :], 0.125 * m_ref[:, rows - 1, :]
    factor_w = 1.0 - (top_e + top_w)
    factor_a = 1.0 - (top_e + top_a)

    at_row = lax.broadcasted_iota(jnp.int32, (count, LANES), 0)
    at_lane = lax.broadcasted_iota(jnp.int32, (count, LANES), 1)
    on_edge = ((at_row < planes) & (at_lane == 0)) | (
        (at_row >= count - planes) & (at_lane == LANES - 1)
    )

    def spread_edge(value):
        value = jnp.sum(value, axis=1, keepdims=True)
        if count > 2 * planes:
            gap = jnp.zeros((count - 2 * planes, 1), f32)
            value = jnp.concatenate([value[0:planes], gap, value[planes:]], axis=0)
        return jnp.where(on_edge, value, 0.0)

    wait_halos(hr_sem, hxr_ref, hyr_ref)
    sides = hyr_ref[...]
    shift_low, shift_high = m_first * hxr_ref[0], m_last * hxr_ref[1]
    rgx[ix, 0] = (sum_u + spread_edge(sides * edge_q)) + (
        top_e * shift_low + factor_w * shift_high
    )
    rgx[ix, 1] = (sum_a + spread_edge(sides * edge_p)) + (
        factor_a * shift_low + top_e * shift_high
    )
    got_rx = exchange(rgx, 2, ix, nx, True)

    for p in range(planes):
        for j in range(tiles):
            mt_ref[p, pl.ds(j * LANES, LANES), :] = m_ref[j * planes + p].T
    joined, nodes_y = sweep_coefficients(mt_ref, ry_ref, ey_ref, turns, ly)
    for c in range(3):
        cgy[iy, c] = joined[c]
    got_cy = exchange(cgy, 1, iy, ny, False)

    spread = jnp.concatenate([sides, jnp.zeros((LANES - 2 * planes, LANES), f32)], axis=0)
    col_ref[...] = spread.T
    u = total = None
    for g in range(lx):
        at = pl.ds(g, BLOCKS, stride=lx)
        column = 0.125 * col_ref[at, :]
        f = fx_ref[g]
        parts = [f[i] for i in range(count)]
        for p in range(planes):
            low = column if p == 0 else pltpu.roll(column, LANES - p, 1)
            high = pltpu.roll(column, LANES - 1 - planes - p, 1)
            i = p
            parts[i] = parts[i] + jnp.where(lane1 == 0, low, 0.0) * m_ref[i, at, :]
            i = (tiles - 1) * planes + p
            parts[i] = parts[i] + jnp.where(lane1 == LANES - 1, high, 0.0) * m_ref[i, at, :]
        f = jnp.stack(parts)
        u = (f if g == 0 else f + u) * rx_ref[g]
        total = u if g == 0 else total + ex_ref[g - 1] * u
        ux_ref[g] = u

    def store_x(g, value):
        vx_ref[g] = value

    own_solution(u, total, nodes_x, count, lx, rx_ref, ex_ref, ux_ref, turns, store_x)

    def store_responses_y(g, e, w):
        at = pl.ds(g, BLOCKS, stride=ly)
        py_ref[:, at, :] = e
        qy_ref[:, at, :] = w

    responses(nodes_y, planes, ly, ry_ref, ey_ref, turns, store_responses_y)
    for p in range(planes):
        for j in range(tiles):
            at = pl.ds(j * LANES, LANES)
            m = mt_ref[p, at, :]
            pm_ref[j * planes + p] = (m * py_ref[p, at, :]).T
            qm_ref[j * planes + p] = (m * qy_ref[p, at, :]).T
    for g in range(lx):
        at = pl.ds(g, BLOCKS, stride=lx)
        pf_ref[g] = pm_ref[:, at, :]
        qf_ref[g] = qm_ref[:, at, :]
    got_cx.wait()
    interface_weights(cgx, ix, nx, sidex, weightx)

    got_rx.wait()
    low, high = outer_values(rgx, weightx, nx)
    low = jnp.broadcast_to((low + shift_low)[:, None, :], shape)
    high = jnp.broadcast_to((high + shift_high)[:, None, :], shape)
    lane_of = lax.broadcasted_iota(jnp.int32, (planes, BLOCKS, LANES), 2)
    block_of = lax.broadcasted_iota(jnp.int32, (planes, BLOCKS, LANES), 1)
    sum_u = jnp.zeros((planes, BLOCKS, LANES), f32)
    sum_a = sum_u
    for g in range(lx):
        v = (vx_ref[g] + px_ref[g] * low) + qx_ref[g] * high
        mid_ref[:, pl.ds(g, BLOCKS, stride=lx), :] = v
        of_u = jnp.sum((v * qf_ref[g]).reshape(tiles, planes, BLOCKS, LANES), axis=0)
        of_a = jnp.sum((v * pf_ref[g]).reshape(tiles, planes, BLOCKS, LANES), axis=0)
        here = lax.rem(lane_of, lx) == g
        sum_u = jnp.where(here, jnp.sum(of_u, axis=2, keepdims=True), sum_u)
        sum_a = jnp.where(here, jnp.sum(of_a, axis=2, keepdims=True), sum_a)
    diagonal = lax.div(lane_of, lx) == block_of
    rgy[iy, 0] = jnp.sum(jnp.where(diagonal, sum_u, 0.0), axis=1)
    rgy[iy, 1] = jnp.sum(jnp.where(diagonal, sum_a, 0.0), axis=1)
    got_ry = exchange(rgy, 3, iy, ny, False)

    for p in range(planes):
        for j in range(tiles):
            midt_ref[p, pl.ds(j * LANES, LANES), :] = mid_ref[j * planes + p].T
    u = total = None
    for g in range(ly):
        at = pl.ds(g, BLOCKS, stride=ly)
        f = midt_ref[:, at, :] * mt_ref[:, at, :]
        u = (f if g == 0 else f + u) * ry_ref[g]
        total = u if g == 0 else total + ey_ref[g - 1] * u
        uy_ref[g] = u

    def store_y(g, value):
        midt_ref[:, pl.ds(g, BLOCKS, stride=ly), :] = value

    own_solution(u, total, nodes_y, planes, ly, ry_ref, ey_ref, uy_ref, turns, store_y)
    got_cy.wait()
    interface_weights(cgy, iy, ny, sidey, weighty)
    wait_halos(hs_sem, hxs_ref, hys_ref)
    for copy in sent[:-1]:
        copy.wait()

    got_ry.wait()
    low, high = outer_values(rgy, weighty, ny)
    for p in range(planes):
        for j in range(tiles):
            at = pl.ds(j * LANES, LANES)
            value = midt_ref[p, at, :] + py_ref[p, at, :] * low[p : p + 1]
            value = value + qy_ref[p, at, :] * high[p : p + 1]
            out_ref[p, :, at] = value.T
    sent[-1].wait()


def on_device(nx, ny, initial_heat_state, spreading_coefficient):
    planes, rows, columns = initial_heat_state.shape
    count = planes * (columns // LANES)
    lx = rows // BLOCKS
    ly = columns // BLOCKS

    def vmem(*shape):
        return pltpu.VMEM(shape, jnp.float32)

    def dma(number):
        return pltpu.SemaphoreType.DMA((number,))

    natural = vmem(count, rows, LANES)
    turned = vmem(planes, columns, LANES)
    steps_x = vmem(lx, count, BLOCKS, LANES)
    steps_y = vmem(ly, planes, BLOCKS, LANES)
    return pl.pallas_call(
        functools.partial(kernel, nx, ny),
        out_shape=jax.ShapeDtypeStruct((planes, rows, columns), jnp.float32),
        in_specs=[pl.BlockSpec(memory_space=pltpu.HBM)] * 2,
        out_specs=pl.BlockSpec(memory_space=pltpu.VMEM),
        scratch_shapes=[
            natural,
            natural,
            natural,
            turned,
            steps_x,
            steps_x,
            steps_x,
            steps_x,
            steps_x,
            steps_x,
            steps_x,
            natural,
            natural,
            steps_y,
            steps_y,
            steps_y,
            turned,
            turned,
            steps_x,
            steps_x,
            natural,
            turned,
            vmem(count * BLOCKS, LANES),
            vmem(count * BLOCKS, LANES),
            vmem(count * BLOCKS, LANES),
            vmem(count * BLOCKS, LANES),
            vmem(2, count, LANES),
            vmem(2, count, LANES),
            vmem(2 * planes, LANES),
            vmem(2 * planes, LANES),
            vmem(rows, LANES),
            vmem(nx, 3, count, LANES),
            vmem(nx, 2, count, LANES),
            vmem(ny, 3, planes, LANES),
            vmem(ny, 2, planes, LANES),
            vmem(6, nx + 1, count, LANES),
            vmem(6, ny + 1, planes, LANES),
            vmem(nx, 4, count, LANES),
            vmem(ny, 4, planes, LANES),
            dma(2),
            dma(2),
            dma(2),
            dma(4),
            dma(4),
        ],
        compiler_params=pltpu.CompilerParams(
            collective_id=0, has_side_effects=True, vmem_limit_bytes=32 << 20
        ),
    )(
        pltpu.with_memory_space_constraint(initial_heat_state, pltpu.HBM),
        pltpu.with_memory_space_constraint(spreading_coefficient, pltpu.HBM),
    )


def solution(mesh):
    return jax.shard_map(
        functools.partial(on_device, mesh.shape["px"], mesh.shape["py"]),
        mesh=mesh,
        in_specs=(P(None, "px", "py"), P(None, "px", "py")),
        out_specs=P(None, "px", "py"),
        check_vma=False,
    )
```

```python
import functools

import jax
import jax.numpy as jnp
from jax import lax
from jax.experimental import pallas as pl
from jax.experimental.pallas import tpu as pltpu
from jax.sharding import PartitionSpec as P

LANES = 128
BLOCKS = 8
MESH = pl.DeviceIdType.MESH


def combine(left, right):
    e_p, w_p, a_p = left
    e_q, w_q, a_q = right
    gap_p = e_p + w_p
    gap_q = e_q + a_q
    r_p = 1.0 - gap_p
    b_q = 1.0 - gap_q
    inv = 1.0 / (gap_p + r_p * gap_q)
    joined = (
        e_p * e_q * inv,
        w_q + e_q * ((w_p + r_p * a_q) * inv),
        a_p + e_p * ((a_q + b_q * w_p) * inv),
    )
    return joined, (inv, r_p, b_q, e_p, e_q)


def combine_rhs(node, left, right):
    inv, r_p, b_q, e_p, e_q = node
    u_p, a_p = left
    u_q, a_q = right
    p0 = (u_p + r_p * a_q) * inv
    q0 = (a_q + b_q * u_p) * inv
    return (u_q + e_q * p0, a_p + e_p * q0), (p0, q0)


def split(node, start, low, high):
    inv, r_p, b_q, e_p, e_q = node
    p = q = None
    if low is not None:
        from_low = e_p * inv * low
        p, q = from_low, b_q * from_low
    if high is not None:
        from_high = e_q * inv * high
        p = r_p * from_high if p is None else p + r_p * from_high
        q = from_high if q is None else q + from_high
    if start is not None:
        p = start[0] if p is None else start[0] + p
        q = start[1] if q is None else start[1] + q
    return p, q


def tree_coefficients(leaves):
    nodes = []
    while len(leaves) > 1:
        pairs = [combine(leaves[i], leaves[i + 1]) for i in range(0, len(leaves), 2)]
        leaves = [pair[0] for pair in pairs]
        nodes.append([pair[1] for pair in pairs])
    return leaves[0], nodes


def tree_up(nodes, leaves):
    starts = []
    for level in nodes:
        pairs = [
            combine_rhs(level[i], leaves[2 * i], leaves[2 * i + 1]) for i in range(len(level))
        ]
        leaves = [pair[0] for pair in pairs]
        starts.append([pair[1] for pair in pairs])
    return leaves[0], starts


def tree_down(nodes, starts, low, high):
    bounds = [(low, high)]
    for depth in range(len(nodes) - 1, -1, -1):
        below = []
        for i, (lo, hi) in enumerate(bounds):
            start = None if starts is None else starts[depth][i]
            p, q = split(nodes[depth][i], start, lo, hi)
            below += [(lo, q), (p, hi)]
        bounds = below
    zero = jnp.zeros_like(nodes[0][0][0])
    return [tuple(zero if x is None else x for x in pair) for pair in bounds]


def leaf_rows(turn_ref, values, count):
    turn_ref[0 : count * BLOCKS, :] = values.reshape(count * BLOCKS, LANES)
    return [turn_ref[pl.ds(b, count, stride=BLOCKS), :] for b in range(BLOCKS)]


def block_rows(turn_ref, rows, count):
    for b in range(BLOCKS):
        turn_ref[pl.ds(b, count, stride=BLOCKS), :] = rows[b]
    return turn_ref[0 : count * BLOCKS, :].reshape(count, BLOCKS, LANES)


def sweep_coefficients(m_ref, r_ref, e_ref, turn_refs, length):
    count = m_ref.shape[0]
    for g in range(length):
        m = m_ref[:, pl.ds(g, BLOCKS, stride=length), :]
        if g == 0:
            t = 1.0 + m
            r = 1.0 / (1.0 + t)
            e = r
            w = m * r
            a = w
        else:
            t = m + t * r
            r = 1.0 / (1.0 + t)
            w = (m + w) * r
            a = a + e * w
            e = e * r
        r_ref[g] = r
        e_ref[g] = e
    leaves = [leaf_rows(ref, value, count) for ref, value in zip(turn_refs, (e, w, a))]
    return tree_coefficients([tuple(leaf[b] for leaf in leaves) for b in range(BLOCKS)])


def responses(nodes, count, length, r_ref, e_ref, turns, store):
    one = jnp.ones((count, LANES), jnp.float32)
    bounds = tree_down(nodes, None, one, None)
    low_e = block_rows(turns[0], [b[0] for b in bounds], count)
    value_e = block_rows(turns[1], [b[1] for b in bounds], count)
    bounds = tree_down(nodes, None, None, one)
    low_w = block_rows(turns[2], [b[0] for b in bounds], count)
    value_w = block_rows(turns[3], [b[1] for b in bounds], count)
    for g in range(length - 1, -1, -1):
        e, r = e_ref[g], r_ref[g]
        value_e = e * low_e + r * value_e
        value_w = e * low_w + r * value_w
        store(g, value_e, value_w)


def own_solution(u, total, nodes, count, length, r_ref, e_ref, u_ref, turns, store):
    leaves = [leaf_rows(ref, value, count) for ref, value in zip(turns, (u, total))]
    _, starts = tree_up(nodes, list(zip(*leaves)))
    bounds = tree_down(nodes, starts, None, None)
    low = block_rows(turns[0], [b[0] for b in bounds], count)
    value = block_rows(turns[1], [b[1] for b in bounds], count)
    for g in range(length - 1, -1, -1):
        value = (u_ref[g] + e_ref[g] * low) + r_ref[g] * value
        store(g, value)


def interface_weights(gathered, me, n, side_ref, weight_ref):
    blocks = [tuple(gathered[i, c] for c in range(3)) for i in range(n)]
    zero = jnp.zeros_like(blocks[0][0])
    one = jnp.ones_like(zero)
    side_ref[0, 0], side_ref[1, 0] = zero, one
    side_ref[2, n], side_ref[3, n] = zero, one
    total = None
    factor, gap = zero, one
    up = []
    for j in range(n):
        e, w, a = blocks[j]
        t = e / (gap + factor * (e + a))
        up.append((t, factor))
        side_ref[4, j] = t
        total = blocks[j] if total is None else combine(total, blocks[j])[0]
        gap = total[0] + total[1]
        factor = 1.0 - gap
        side_ref[0, j + 1], side_ref[1, j + 1] = factor, gap
    total = None
    factor, gap = zero, one
    down = [None] * n
    for j in range(n - 1, -1, -1):
        e, w, a = blocks[j]
        s = e / ((e + w) + (1.0 - (e + w)) * gap)
        down[j] = (s, factor)
        side_ref[5, j] = s
        total = blocks[j] if total is None else combine(blocks[j], total)[0]
        gap = total[0] + total[2]
        factor = 1.0 - gap
        side_ref[2, j], side_ref[3, j] = factor, gap
    below, above = side_ref[0, me], side_ref[2, me + 1]
    at_low = 1.0 / (side_ref[1, me] + below * side_ref[3, me])
    at_high = 1.0 / (side_ref[1, me + 1] + side_ref[0, me + 1] * side_ref[3, me + 1])
    t, s = side_ref[4, me], side_ref[5, me]
    low_x, low_y = at_low, at_low * below * s
    high_x, high_y = at_high * above * t, at_high
    through = one
    for j in range(n - 1, -1, -1):
        inside = j < me
        keep = jnp.where(inside, through, 0.0)
        t_j, factor_j = up[j]
        other = keep * (t_j * factor_j)
        weight_ref[j, 0], weight_ref[j, 1] = low_x * keep, low_x * other
        weight_ref[j, 2], weight_ref[j, 3] = high_x * keep, high_x * other
        through = jnp.where(inside, through * t_j, through)
    through = one
    for j in range(n):
        inside = j > me
        keep = jnp.where(inside, through, 0.0)
        s_j, factor_j = down[j]
        other = keep * (s_j * factor_j)
        weight_ref[j, 0] += low_y * other
        weight_ref[j, 1] += low_y * keep
        weight_ref[j, 2] += high_y * other
        weight_ref[j, 3] += high_y * keep
        through = jnp.where(inside, through * s_j, through)
    weight_ref[me, 0] = low_y * above
    weight_ref[me, 1] = at_low * below
    weight_ref[me, 2] = at_high * above
    weight_ref[me, 3] = high_x * below


def outer_values(gathered, weight_ref, n):
    low, high = [], []
    for j in range(n):
        u, a = gathered[j, 0], gathered[j, 1]
        low.append(weight_ref[j, 0] * u + weight_ref[j, 1] * a)
        high.append(weight_ref[j, 2] * u + weight_ref[j, 3] * a)
    while len(low) > 1:
        low = [sum(low[i : i + 2]) for i in range(0, len(low), 2)]
        high = [sum(high[i : i + 2]) for i in range(0, len(high), 2)]
    return low[0], high[0]


def partner(me, d, n):
    if n & (n - 1):
        return lax.rem(me + d, n)
    at, b = me, 1
    while b < n:
        if d & b:
            at = at + b - 2 * b * lax.rem(lax.div(me, b), 2)
        b *= 2
    return at


def far_first(n):
    return sorted(range(1, n), key=lambda d: (-(d // 2), d % 2))


def kernel(
    nx,
    ny,
    h_hbm,
    k_hbm,
    out_ref,
    k_ref,
    h_ref,
    m_ref,
    mt_ref,
    rx_ref,
    ex_ref,
    ux_ref,
    fx_ref,
    vx_ref,
    px_ref,
    qx_ref,
    pm_ref,
    qm_ref,
    ry_ref,
    ey_ref,
    uy_ref,
    py_ref,
    qy_ref,
    pf_ref,
    qf_ref,
    mid_ref,
    midt_ref,
    turn0,
    turn1,
    turn2,
    turn3,
    hxs_ref,
    hxr_ref,
    hys_ref,
    hyr_ref,
    col_ref,
    cgx,
    rgx,
    cgy,
    rgy,
    sidex,
    sidey,
    weightx,
    weighty,
    in_sem,
    hs_sem,
    hr_sem,
    ps_sem,
    pr_sem,
):
    ix = lax.axis_index("px")
    iy = lax.axis_index("py")
    planes, rows, columns = h_hbm.shape
    tiles = columns // LANES
    count = tiles * planes
    lx = rows // BLOCKS
    ly = columns // BLOCKS
    turns = (turn0, turn1, turn2, turn3)
    f32 = jnp.float32

    def stage(source, target, number):
        for j in range(tiles):
            pltpu.make_async_copy(
                source.at[:, :, pl.ds(j * LANES, LANES)],
                target.at[pl.ds(j * planes, planes)],
                in_sem.at[number],
            ).start()
        return pltpu.make_async_copy(target, target, in_sem.at[number])

    barrier = pltpu.get_barrier_semaphore()
    for d in range(ny - 1, 0, -1):
        pl.semaphore_signal(barrier, inc=1, device_id=(ix, partner(iy, d, ny)), device_id_type=MESH)
    for d in far_first(nx):
        pl.semaphore_signal(barrier, inc=1, device_id=(partner(ix, d, nx), iy), device_id_type=MESH)

    staged_h = stage(h_hbm, h_ref, 0)
    staged_k = stage(k_hbm, k_ref, 1)

    sent = []

    def exchange(ref, number, me, n, along_x):
        def push(to):
            return pltpu.make_async_remote_copy(
                src_ref=ref.at[me],
                dst_ref=ref.at[me],
                send_sem=ps_sem.at[number],
                recv_sem=pr_sem.at[number],
                device_id=(to, iy) if along_x else (ix, to),
                device_id_type=MESH,
            ).start

        pl.when(me > 0)(push(0))
        for d in far_first(n) if along_x else range(n - 1, 0, -1):
            to = partner(me, d, n)
            pl.when(to > 0)(push(to))
        others = ref.at[pl.ds(0, n - 1)]
        sent.append(pltpu.make_async_copy(others, others, ps_sem.at[number]))
        return pltpu.make_async_copy(others, others, pr_sem.at[number])

    @pl.when(ix == 0)
    def _():
        hxr_ref[0] = jnp.zeros_like(hxr_ref[0])

    @pl.when(ix == nx - 1)
    def _():
        hxr_ref[1] = jnp.zeros_like(hxr_ref[1])

    low_side = pl.ds(0, planes)
    high_side = pl.ds(planes, planes)

    @pl.when(iy == 0)
    def _():
        hyr_ref[low_side] = jnp.zeros((planes, LANES), f32)

    @pl.when(iy == ny - 1)
    def _():
        hyr_ref[high_side] = jnp.zeros((planes, LANES), f32)

    def halo(source, target, number, device):
        return pltpu.make_async_remote_copy(
            src_ref=source,
            dst_ref=target,
            send_sem=hs_sem.at[number],
            recv_sem=hr_sem.at[number],
            device_id=device,
            device_id_type=MESH,
        )

    x_down = halo(hxs_ref.at[0], hxr_ref.at[1], 0, (lax.rem(ix + nx - 1, nx), iy))
    x_up = halo(hxs_ref.at[1], hxr_ref.at[0], 0, (lax.rem(ix + 1, nx), iy))
    y_down = halo(
        hys_ref.at[low_side], hyr_ref.at[high_side], 1, (ix, lax.rem(iy + ny - 1, ny))
    )
    y_up = halo(hys_ref.at[high_side], hyr_ref.at[low_side], 1, (ix, lax.rem(iy + 1, ny)))
    routes = (
        (y_down, iy > 0),
        (y_up, iy < ny - 1),
        (x_down, ix > 0),
        (x_up, ix < nx - 1),
    )

    def wait_halos(sem, x_ref, y_ref):
        inner_x = (ix > 0) & (ix < nx - 1)
        inner_y = (iy > 0) & (iy < ny - 1)
        for ref, part, number, inner in (
            (x_ref, x_ref.at[0], 0, inner_x),
            (y_ref, y_ref.at[low_side], 1, inner_y),
        ):
            pl.when(inner)(pltpu.make_async_copy(ref, ref, sem.at[number]).wait)
            pl.when(jnp.logical_not(inner))(pltpu.make_async_copy(part, part, sem.at[number]).wait)

    lane = lax.broadcasted_iota(jnp.int32, (rows, LANES), 1)

    def edge_columns(ref):
        packed = jnp.zeros((rows, LANES), f32)
        for p in range(planes):
            low = ref[p]
            high = ref[(tiles - 1) * planes + p]
            packed = jnp.where(lane == p, low if p == 0 else pltpu.roll(low, p, 1), packed)
            packed = jnp.where(lane == planes + p, pltpu.roll(high, planes + p + 1, 1), packed)
        return packed.T[0 : 2 * planes]

    staged_h.wait()
    hxs_ref[0] = h_ref[:, 0, :]
    hxs_ref[1] = h_ref[:, rows - 1, :]
    hys_ref[...] = edge_columns(h_ref)

    pl.semaphore_wait(barrier, nx + ny - 2)
    for copy, sends in routes:
        pl.when(sends)(copy.start)

    staged_k.wait()
    m_ref[...] = 1.0 / k_ref[...]
    joined, nodes_x = sweep_coefficients(m_ref, rx_ref, ex_ref, turns, lx)
    for c in range(3):
        cgx[ix, c] = joined[c]
    got_cx = exchange(cgx, 0, ix, nx, True)
    top_e, top_w, top_a = joined

    def store_responses_x(g, e, w):
        px_ref[g], qx_ref[g] = e, w
        at = pl.ds(g, BLOCKS, stride=lx)
        m = 0.125 * m_ref[:, at, :]
        pm_ref[:, at, :] = m * e
        qm_ref[:, at, :] = m * w

    responses(nodes_x, count, lx, rx_ref, ex_ref, turns, store_responses_x)
    edge_p, edge_q = edge_columns(pm_ref), edge_columns(qm_ref)

    def field(g):
        return h_ref[:, pl.ds(g, BLOCKS, stride=lx), :]

    shape = (count, BLOCKS, LANES)
    sub = lax.broadcasted_iota(jnp.int32, shape, 1)
    lane1 = lax.broadcasted_iota(jnp.int32, (BLOCKS, LANES), 1)
    none = jnp.zeros((BLOCKS, LANES), f32)
    now = field(0)
    before = jnp.where(sub == 0, 0.0, pltpu.roll(field(lx - 1), 1, 1))
    beyond = jnp.where(sub == BLOCKS - 1, 0.0, pltpu.roll(now, BLOCKS - 1, 1))
    sum_u = sum_a = None
    for g in range(lx):
        after = field(g + 1) if g + 1 < lx else beyond
        to_right = pltpu.roll(now, 1, 2)
        to_left = pltpu.roll(now, LANES - 1, 2)
        around = []
        for j in range(tiles):
            for p in range(planes):
                i = j * planes + p
                low = none if j == 0 else to_right[i - planes]
                high = none if j == tiles - 1 else to_left[i + planes]
                left = jnp.where(lane1 == 0, low, to_right[i])
                right = jnp.where(lane1 == LANES - 1, high, to_left[i])
                under = now[i - 1] if p > 0 else none
                over = now[i + 1] if p < planes - 1 else none
                around.append((over + under) + (left + right))
        around = jnp.stack(around) + (after + before)
        source = now + 0.125 * (around - 6.0 * now)
        f = source * m_ref[:, pl.ds(g, BLOCKS, stride=lx), :]
        fx_ref[g] = f
        sum_u = f * qx_ref[g] if g == 0 else sum_u + f * qx_ref[g]
        sum_a = f * px_ref[g] if g == 0 else sum_a + f * px_ref[g]
        before, now = now, after
    sum_u, sum_a = jnp.sum(sum_u, axis=1), jnp.sum(sum_a, axis=1)
    m_first, m_last = 0.125 * m_ref[:, 0, :], 0.125 * m_ref[:, rows - 1, :]
    factor_w = 1.0 - (top_e + top_w)
    factor_a = 1.0 - (top_e + top_a)

    at_row = lax.broadcasted_iota(jnp.int32, (count, LANES), 0)
    at_lane = lax.broadcasted_iota(jnp.int32, (count, LANES), 1)
    on_edge = ((at_row < planes) & (at_lane == 0)) | (
        (at_row >= count - planes) & (at_lane == LANES - 1)
    )

    def spread_edge(value):
        value = jnp.sum(value, axis=1, keepdims=True)
        if count > 2 * planes:
            gap = jnp.zeros((count - 2 * planes, 1), f32)
            value = jnp.concatenate([value[0:planes], gap, value[planes:]], axis=0)
        return jnp.where(on_edge, value, 0.0)

    wait_halos(hr_sem, hxr_ref, hyr_ref)
    sides = hyr_ref[...]
    shift_low, shift_high = m_first * hxr_ref[0], m_last * hxr_ref[1]
    rgx[ix, 0] = (sum_u + spread_edge(sides * edge_q)) + (
        top_e * shift_low + factor_w * shift_high
    )
    rgx[ix, 1] = (sum_a + spread_edge(sides * edge_p)) + (
        factor_a * shift_low + top_e * shift_high
    )
    got_rx = exchange(rgx, 2, ix, nx, True)

    for p in range(planes):
        for j in range(tiles):
            mt_ref[p, pl.ds(j * LANES, LANES), :] = m_ref[j * planes + p].T
    joined, nodes_y = sweep_coefficients(mt_ref, ry_ref, ey_ref, turns, ly)
    for c in range(3):
        cgy[iy, c] = joined[c]
    got_cy = exchange(cgy, 1, iy, ny, False)

    spread = jnp.concatenate([sides, jnp.zeros((LANES - 2 * planes, LANES), f32)], axis=0)
    col_ref[...] = spread.T
    u = total = None
    for g in range(lx):
        at = pl.ds(g, BLOCKS, stride=lx)
        column = 0.125 * col_ref[at, :]
        f = fx_ref[g]
        parts = [f[i] for i in range(count)]
        for p in range(planes):
            low = column if p == 0 else pltpu.roll(column, LANES - p, 1)
            high = pltpu.roll(column, LANES - 1 - planes - p, 1)
            i = p
            parts[i] = parts[i] + jnp.where(lane1 == 0, low, 0.0) * m_ref[i, at, :]
            i = (tiles - 1) * planes + p
            parts[i] = parts[i] + jnp.where(lane1 == LANES - 1, high, 0.0) * m_ref[i, at, :]
        f = jnp.stack(parts)
        u = (f if g == 0 else f + u) * rx_ref[g]
        total = u if g == 0 else total + ex_ref[g - 1] * u
        ux_ref[g] = u

    def store_x(g, value):
        vx_ref[g] = value

    own_solution(u, total, nodes_x, count, lx, rx_ref, ex_ref, ux_ref, turns, store_x)

    def store_responses_y(g, e, w):
        at = pl.ds(g, BLOCKS, stride=ly)
        py_ref[:, at, :] = e
        qy_ref[:, at, :] = w

    responses(nodes_y, planes, ly, ry_ref, ey_ref, turns, store_responses_y)
    for p in range(planes):
        for j in range(tiles):
            at = pl.ds(j * LANES, LANES)
            m = mt_ref[p, at, :]
            pm_ref[j * planes + p] = (m * py_ref[p, at, :]).T
            qm_ref[j * planes + p] = (m * qy_ref[p, at, :]).T
    for g in range(lx):
        at = pl.ds(g, BLOCKS, stride=lx)
        pf_ref[g] = pm_ref[:, at, :]
        qf_ref[g] = qm_ref[:, at, :]
    row_of = lax.broadcasted_iota(jnp.int32, (BLOCKS, LANES), 0)
    here = [lax.rem(lane1, lx) == g for g in range(lx)]
    diagonal = lax.div(lane1, lx) == row_of

    def line_sums(step):
        rows_u = rows_a = jnp.zeros((planes, BLOCKS, LANES), f32)
        for g in range(lx):
            v = step(g)
            of_u = jnp.sum((v * qf_ref[g]).reshape(tiles, planes, BLOCKS, LANES), axis=0)
            of_a = jnp.sum((v * pf_ref[g]).reshape(tiles, planes, BLOCKS, LANES), axis=0)
            rows_u = jnp.where(here[g][None], jnp.sum(of_u, axis=2, keepdims=True), rows_u)
            rows_a = jnp.where(here[g][None], jnp.sum(of_a, axis=2, keepdims=True), rows_a)
        return [jnp.sum(jnp.where(diagonal[None], r, 0.0), axis=1) for r in (rows_u, rows_a)]

    own_sums = line_sums(lambda g: vx_ref[g])
    got_cx.wait()
    interface_weights(cgx, ix, nx, sidex, weightx)

    got_rx.wait()
    low, high = outer_values(rgx, weightx, nx)
    low = jnp.broadcast_to((low + shift_low)[:, None, :], shape)
    high = jnp.broadcast_to((high + shift_high)[:, None, :], shape)
    sums = line_sums(lambda g: px_ref[g] * low + qx_ref[g] * high)
    for c in range(2):
        rgy[iy, c] = own_sums[c] + sums[c]
    got_ry = exchange(rgy, 3, iy, ny, False)

    for g in range(lx):
        v = (vx_ref[g] + px_ref[g] * low) + qx_ref[g] * high
        mid_ref[:, pl.ds(g, BLOCKS, stride=lx), :] = v
    for p in range(planes):
        for j in range(tiles):
            midt_ref[p, pl.ds(j * LANES, LANES), :] = mid_ref[j * planes + p].T
    u = total = None
    for g in range(ly):
        at = pl.ds(g, BLOCKS, stride=ly)
        f = midt_ref[:, at, :] * mt_ref[:, at, :]
        u = (f if g == 0 else f + u) * ry_ref[g]
        total = u if g == 0 else total + ey_ref[g - 1] * u
        uy_ref[g] = u

    def store_y(g, value):
        midt_ref[:, pl.ds(g, BLOCKS, stride=ly), :] = value

    own_solution(u, total, nodes_y, planes, ly, ry_ref, ey_ref, uy_ref, turns, store_y)
    got_cy.wait()
    interface_weights(cgy, iy, ny, sidey, weighty)
    wait_halos(hs_sem, hxs_ref, hys_ref)
    for copy in sent[:-1]:
        copy.wait()

    got_ry.wait()
    low, high = outer_values(rgy, weighty, ny)
    for p in range(planes):
        for j in range(tiles):
            at = pl.ds(j * LANES, LANES)
            value = midt_ref[p, at, :] + py_ref[p, at, :] * low[p : p + 1]
            value = value + qy_ref[p, at, :] * high[p : p + 1]
            out_ref[p, :, at] = value.T
    sent[-1].wait()


def on_device(nx, ny, initial_heat_state, spreading_coefficient):
    planes, rows, columns = initial_heat_state.shape
    count = planes * (columns // LANES)
    lx = rows // BLOCKS
    ly = columns // BLOCKS

    def vmem(*shape):
        return pltpu.VMEM(shape, jnp.float32)

    def dma(number):
        return pltpu.SemaphoreType.DMA((number,))

    natural = vmem(count, rows, LANES)
    turned = vmem(planes, columns, LANES)
    steps_x = vmem(lx, count, BLOCKS, LANES)
    steps_y = vmem(ly, planes, BLOCKS, LANES)
    return pl.pallas_call(
        functools.partial(kernel, nx, ny),
        out_shape=jax.ShapeDtypeStruct((planes, rows, columns), jnp.float32),
        in_specs=[pl.BlockSpec(memory_space=pltpu.HBM)] * 2,
        out_specs=pl.BlockSpec(memory_space=pltpu.VMEM),
        scratch_shapes=[
            natural,
            natural,
            natural,
            turned,
            steps_x,
            steps_x,
            steps_x,
            steps_x,
            steps_x,
            steps_x,
            steps_x,
            natural,
            natural,
            steps_y,
            steps_y,
            steps_y,
            turned,
            turned,
            steps_x,
            steps_x,
            natural,
            turned,
            vmem(count * BLOCKS, LANES),
            vmem(count * BLOCKS, LANES),
            vmem(count * BLOCKS, LANES),
            vmem(count * BLOCKS, LANES),
            vmem(2, count, LANES),
            vmem(2, count, LANES),
            vmem(2 * planes, LANES),
            vmem(2 * planes, LANES),
            vmem(rows, LANES),
            vmem(nx, 3, count, LANES),
            vmem(nx, 2, count, LANES),
            vmem(ny, 3, planes, LANES),
            vmem(ny, 2, planes, LANES),
            vmem(6, nx + 1, count, LANES),
            vmem(6, ny + 1, planes, LANES),
            vmem(nx, 4, count, LANES),
            vmem(ny, 4, planes, LANES),
            dma(2),
            dma(2),
            dma(2),
            dma(4),
            dma(4),
        ],
        compiler_params=pltpu.CompilerParams(
            collective_id=0, has_side_effects=True, vmem_limit_bytes=32 << 20
        ),
    )(
        pltpu.with_memory_space_constraint(initial_heat_state, pltpu.HBM),
        pltpu.with_memory_space_constraint(spreading_coefficient, pltpu.HBM),
    )


def solution(mesh):
    return jax.shard_map(
        functools.partial(on_device, mesh.shape["px"], mesh.shape["py"]),
        mesh=mesh,
        in_specs=(P(None, "px", "py"), P(None, "px", "py")),
        out_specs=P(None, "px", "py"),
        check_vma=False,
    )
```

```python
import functools

import jax
import jax.numpy as jnp
from jax import lax
from jax.experimental import pallas as pl
from jax.experimental.pallas import tpu as pltpu
from jax.sharding import PartitionSpec as P

LANES = 128
BLOCKS = 8
MESH = pl.DeviceIdType.MESH


def combine(left, right):
    e_p, w_p, a_p = left
    e_q, w_q, a_q = right
    gap_p = e_p + w_p
    gap_q = e_q + a_q
    r_p = 1.0 - gap_p
    b_q = 1.0 - gap_q
    inv = 1.0 / (gap_p + r_p * gap_q)
    joined = (
        e_p * e_q * inv,
        w_q + e_q * ((w_p + r_p * a_q) * inv),
        a_p + e_p * ((a_q + b_q * w_p) * inv),
    )
    return joined, (inv, r_p, b_q, e_p, e_q)


def combine_rhs(node, left, right):
    inv, r_p, b_q, e_p, e_q = node
    u_p, a_p = left
    u_q, a_q = right
    p0 = (u_p + r_p * a_q) * inv
    q0 = (a_q + b_q * u_p) * inv
    return (u_q + e_q * p0, a_p + e_p * q0), (p0, q0)


def split(node, start, low, high):
    inv, r_p, b_q, e_p, e_q = node
    p = q = None
    if low is not None:
        from_low = e_p * inv * low
        p, q = from_low, b_q * from_low
    if high is not None:
        from_high = e_q * inv * high
        p = r_p * from_high if p is None else p + r_p * from_high
        q = from_high if q is None else q + from_high
    if start is not None:
        p = start[0] if p is None else start[0] + p
        q = start[1] if q is None else start[1] + q
    return p, q


def tree_coefficients(leaves):
    nodes = []
    while len(leaves) > 1:
        pairs = [combine(leaves[i], leaves[i + 1]) for i in range(0, len(leaves), 2)]
        leaves = [pair[0] for pair in pairs]
        nodes.append([pair[1] for pair in pairs])
    return leaves[0], nodes


def tree_up(nodes, leaves):
    starts = []
    for level in nodes:
        pairs = [
            combine_rhs(level[i], leaves[2 * i], leaves[2 * i + 1]) for i in range(len(level))
        ]
        leaves = [pair[0] for pair in pairs]
        starts.append([pair[1] for pair in pairs])
    return leaves[0], starts


def tree_down(nodes, starts, low, high):
    bounds = [(low, high)]
    for depth in range(len(nodes) - 1, -1, -1):
        below = []
        for i, (lo, hi) in enumerate(bounds):
            start = None if starts is None else starts[depth][i]
            p, q = split(nodes[depth][i], start, lo, hi)
            below += [(lo, q), (p, hi)]
        bounds = below
    zero = jnp.zeros_like(nodes[0][0][0])
    return [tuple(zero if x is None else x for x in pair) for pair in bounds]


def leaf_rows(turn_ref, values, count):
    turn_ref[0 : count * BLOCKS, :] = values.reshape(count * BLOCKS, LANES)
    return [turn_ref[pl.ds(b, count, stride=BLOCKS), :] for b in range(BLOCKS)]


def block_rows(turn_ref, rows, count):
    for b in range(BLOCKS):
        turn_ref[pl.ds(b, count, stride=BLOCKS), :] = rows[b]
    return turn_ref[0 : count * BLOCKS, :].reshape(count, BLOCKS, LANES)


def sweep_coefficients(m_ref, r_ref, e_ref, turn_refs, length):
    count = m_ref.shape[0]
    for g in range(length):
        m = m_ref[:, pl.ds(g, BLOCKS, stride=length), :]
        if g == 0:
            t = 1.0 + m
            r = 1.0 / (1.0 + t)
            e = r
            w = m * r
            a = w
        else:
            t = m + t * r
            r = 1.0 / (1.0 + t)
            w = (m + w) * r
            a = a + e * w
            e = e * r
        r_ref[g] = r
        e_ref[g] = e
    leaves = [leaf_rows(ref, value, count) for ref, value in zip(turn_refs, (e, w, a))]
    return tree_coefficients([tuple(leaf[b] for leaf in leaves) for b in range(BLOCKS)])


def responses(nodes, count, length, r_ref, e_ref, turns, store):
    one = jnp.ones((count, LANES), jnp.float32)
    bounds = tree_down(nodes, None, one, None)
    low_e = block_rows(turns[0], [b[0] for b in bounds], count)
    value_e = block_rows(turns[1], [b[1] for b in bounds], count)
    bounds = tree_down(nodes, None, None, one)
    low_w = block_rows(turns[2], [b[0] for b in bounds], count)
    value_w = block_rows(turns[3], [b[1] for b in bounds], count)
    for g in range(length - 1, -1, -1):
        e, r = e_ref[g], r_ref[g]
        value_e = e * low_e + r * value_e
        value_w = e * low_w + r * value_w
        store(g, value_e, value_w)


def own_solution(u, total, nodes, count, length, r_ref, e_ref, u_ref, turns, store):
    leaves = [leaf_rows(ref, value, count) for ref, value in zip(turns, (u, total))]
    _, starts = tree_up(nodes, list(zip(*leaves)))
    bounds = tree_down(nodes, starts, None, None)
    low = block_rows(turns[0], [b[0] for b in bounds], count)
    value = block_rows(turns[1], [b[1] for b in bounds], count)
    for g in range(length - 1, -1, -1):
        value = (u_ref[g] + e_ref[g] * low) + r_ref[g] * value
        store(g, value)


def interface_weights(gathered, me, n, side_ref, weight_ref):
    blocks = [tuple(gathered[i, c] for c in range(3)) for i in range(n)]
    zero = jnp.zeros_like(blocks[0][0])
    one = jnp.ones_like(zero)
    side_ref[0, 0], side_ref[1, 0] = zero, one
    side_ref[2, n], side_ref[3, n] = zero, one
    total = None
    factor, gap = zero, one
    up = []
    for j in range(n):
        e, w, a = blocks[j]
        t = e / (gap + factor * (e + a))
        up.append((t, factor))
        side_ref[4, j] = t
        total = blocks[j] if total is None else combine(total, blocks[j])[0]
        gap = total[0] + total[1]
        factor = 1.0 - gap
        side_ref[0, j + 1], side_ref[1, j + 1] = factor, gap
    total = None
    factor, gap = zero, one
    down = [None] * n
    for j in range(n - 1, -1, -1):
        e, w, a = blocks[j]
        s = e / ((e + w) + (1.0 - (e + w)) * gap)
        down[j] = (s, factor)
        side_ref[5, j] = s
        total = blocks[j] if total is None else combine(blocks[j], total)[0]
        gap = total[0] + total[2]
        factor = 1.0 - gap
        side_ref[2, j], side_ref[3, j] = factor, gap
    below, above = side_ref[0, me], side_ref[2, me + 1]
    at_low = 1.0 / (side_ref[1, me] + below * side_ref[3, me])
    at_high = 1.0 / (side_ref[1, me + 1] + side_ref[0, me + 1] * side_ref[3, me + 1])
    t, s = side_ref[4, me], side_ref[5, me]
    low_x, low_y = at_low, at_low * below * s
    high_x, high_y = at_high * above * t, at_high
    through = one
    for j in range(n - 1, -1, -1):
        inside = j < me
        keep = jnp.where(inside, through, 0.0)
        t_j, factor_j = up[j]
        other = keep * (t_j * factor_j)
        weight_ref[j, 0], weight_ref[j, 1] = low_x * keep, low_x * other
        weight_ref[j, 2], weight_ref[j, 3] = high_x * keep, high_x * other
        through = jnp.where(inside, through * t_j, through)
    through = one
    for j in range(n):
        inside = j > me
        keep = jnp.where(inside, through, 0.0)
        s_j, factor_j = down[j]
        other = keep * (s_j * factor_j)
        weight_ref[j, 0] += low_y * other
        weight_ref[j, 1] += low_y * keep
        weight_ref[j, 2] += high_y * other
        weight_ref[j, 3] += high_y * keep
        through = jnp.where(inside, through * s_j, through)
    weight_ref[me, 0] = low_y * above
    weight_ref[me, 1] = at_low * below
    weight_ref[me, 2] = at_high * above
    weight_ref[me, 3] = high_x * below


def outer_values(gathered, weight_ref, n):
    low, high = [], []
    for j in range(n):
        u, a = gathered[j, 0], gathered[j, 1]
        low.append(weight_ref[j, 0] * u + weight_ref[j, 1] * a)
        high.append(weight_ref[j, 2] * u + weight_ref[j, 3] * a)
    while len(low) > 1:
        low = [sum(low[i : i + 2]) for i in range(0, len(low), 2)]
        high = [sum(high[i : i + 2]) for i in range(0, len(high), 2)]
    return low[0], high[0]


def partner(me, d, n):
    if n & (n - 1):
        return lax.rem(me + d, n)
    at, b = me, 1
    while b < n:
        if d & b:
            at = at + b - 2 * b * lax.rem(lax.div(me, b), 2)
        b *= 2
    return at


def far_first(n):
    return sorted(range(1, n), key=lambda d: (-(d // 2), d % 2))


def kernel(
    nx,
    ny,
    h_hbm,
    k_hbm,
    out_ref,
    k_ref,
    h_ref,
    m_ref,
    mt_ref,
    rx_ref,
    ex_ref,
    ux_ref,
    fx_ref,
    vx_ref,
    px_ref,
    qx_ref,
    pm_ref,
    qm_ref,
    ry_ref,
    ey_ref,
    uy_ref,
    py_ref,
    qy_ref,
    pf_ref,
    qf_ref,
    mid_ref,
    midt_ref,
    turn0,
    turn1,
    turn2,
    turn3,
    hxs_ref,
    hxr_ref,
    hys_ref,
    hyr_ref,
    col_ref,
    cgx,
    rgx,
    cgy,
    rgy,
    sidex,
    sidey,
    weightx,
    weighty,
    in_sem,
    hs_sem,
    hr_sem,
    ps_sem,
    pr_sem,
    sent_ref,
):
    ix = lax.axis_index("px")
    iy = lax.axis_index("py")
    planes, rows, columns = h_hbm.shape
    tiles = columns // LANES
    count = tiles * planes
    lx = rows // BLOCKS
    ly = columns // BLOCKS
    turns = (turn0, turn1, turn2, turn3)
    f32 = jnp.float32

    def stage(source, target, number):
        for j in range(tiles):
            pltpu.make_async_copy(
                source.at[:, :, pl.ds(j * LANES, LANES)],
                target.at[pl.ds(j * planes, planes)],
                in_sem.at[number],
            ).start()
        return pltpu.make_async_copy(target, target, in_sem.at[number])

    barrier = pltpu.get_barrier_semaphore()
    for d in range(ny - 1, 0, -1):
        pl.semaphore_signal(barrier, inc=1, device_id=(ix, partner(iy, d, ny)), device_id_type=MESH)
    for d in far_first(nx):
        pl.semaphore_signal(barrier, inc=1, device_id=(partner(ix, d, nx), iy), device_id_type=MESH)

    staged_h = stage(h_hbm, h_ref, 0)
    staged_k = stage(k_hbm, k_ref, 1)

    def exchange(ref, number, me, n, along_x):
        def push(to):
            return pltpu.make_async_remote_copy(
                src_ref=ref.at[me],
                dst_ref=ref.at[me],
                send_sem=ps_sem.at[0],
                recv_sem=pr_sem.at[number],
                device_id=(to, iy) if along_x else (ix, to),
                device_id_type=MESH,
            ).start

        pl.when(me > 0)(push(0))
        for d in far_first(n) if along_x else range(n - 1, 0, -1):
            to = partner(me, d, n)
            pl.when(to > 0)(push(to))
        others = ref.at[pl.ds(0, n - 1)]
        return pltpu.make_async_copy(others, others, pr_sem.at[number])

    @pl.when(ix == 0)
    def _():
        hxr_ref[0] = jnp.zeros_like(hxr_ref[0])

    @pl.when(ix == nx - 1)
    def _():
        hxr_ref[1] = jnp.zeros_like(hxr_ref[1])

    low_side = pl.ds(0, planes)
    high_side = pl.ds(planes, planes)

    @pl.when(iy == 0)
    def _():
        hyr_ref[low_side] = jnp.zeros((planes, LANES), f32)

    @pl.when(iy == ny - 1)
    def _():
        hyr_ref[high_side] = jnp.zeros((planes, LANES), f32)

    def halo(source, target, device):
        return pltpu.make_async_remote_copy(
            src_ref=source,
            dst_ref=target,
            send_sem=hs_sem.at[0],
            recv_sem=hr_sem.at[0],
            device_id=device,
            device_id_type=MESH,
        )

    x_down = halo(hxs_ref.at[0], hxr_ref.at[1], (lax.rem(ix + nx - 1, nx), iy))
    x_up = halo(hxs_ref.at[1], hxr_ref.at[0], (lax.rem(ix + 1, nx), iy))
    y_down = halo(
        hys_ref.at[low_side], hyr_ref.at[high_side], (ix, lax.rem(iy + ny - 1, ny))
    )
    y_up = halo(hys_ref.at[high_side], hyr_ref.at[low_side], (ix, lax.rem(iy + 1, ny)))
    routes = (
        (y_down, iy > 0),
        (y_up, iy < ny - 1),
        (x_down, ix > 0),
        (x_up, ix < nx - 1),
    )

    def wait_halos(sem):
        inner_x = (ix > 0) & (ix < nx - 1)
        inner_y = (iy > 0) & (iy < ny - 1)
        for two_x in (False, True):
            for two_y in (False, True):
                size = (count * (2 if two_x else 1)) + (planes * (2 if two_y else 1))
                part = turn0.at[pl.ds(0, size)]
                here = (inner_x == two_x) & (inner_y == two_y)
                pl.when(here)(pltpu.make_async_copy(part, part, sem).wait)

    lane = lax.broadcasted_iota(jnp.int32, (rows, LANES), 1)

    def edge_columns(ref):
        packed = jnp.zeros((rows, LANES), f32)
        for p in range(planes):
            low = ref[p]
            high = ref[(tiles - 1) * planes + p]
            packed = jnp.where(lane == p, low if p == 0 else pltpu.roll(low, p, 1), packed)
            packed = jnp.where(lane == planes + p, pltpu.roll(high, planes + p + 1, 1), packed)
        return packed.T[0 : 2 * planes]

    staged_h.wait()
    hxs_ref[0] = h_ref[:, 0, :]
    hxs_ref[1] = h_ref[:, rows - 1, :]
    hys_ref[...] = edge_columns(h_ref)

    pl.semaphore_wait(barrier, nx + ny - 2)
    for copy, sends in routes:
        pl.when(sends)(copy.start)

    staged_k.wait()
    m_ref[...] = 1.0 / k_ref[...]
    joined, nodes_x = sweep_coefficients(m_ref, rx_ref, ex_ref, turns, lx)
    for c in range(3):
        cgx[ix, c] = joined[c]
    got_cx = exchange(cgx, 0, ix, nx, True)
    top_e, top_w, top_a = joined

    def store_responses_x(g, e, w):
        px_ref[g], qx_ref[g] = e, w
        at = pl.ds(g, BLOCKS, stride=lx)
        m = 0.125 * m_ref[:, at, :]
        pm_ref[:, at, :] = m * e
        qm_ref[:, at, :] = m * w

    responses(nodes_x, count, lx, rx_ref, ex_ref, turns, store_responses_x)
    edge_p, edge_q = edge_columns(pm_ref), edge_columns(qm_ref)

    def field(g):
        return h_ref[:, pl.ds(g, BLOCKS, stride=lx), :]

    shape = (count, BLOCKS, LANES)
    sub = lax.broadcasted_iota(jnp.int32, shape, 1)
    lane1 = lax.broadcasted_iota(jnp.int32, (BLOCKS, LANES), 1)
    none = jnp.zeros((BLOCKS, LANES), f32)
    now = field(0)
    before = jnp.where(sub == 0, 0.0, pltpu.roll(field(lx - 1), 1, 1))
    beyond = jnp.where(sub == BLOCKS - 1, 0.0, pltpu.roll(now, BLOCKS - 1, 1))
    sum_u = sum_a = None
    for g in range(lx):
        after = field(g + 1) if g + 1 < lx else beyond
        to_right = pltpu.roll(now, 1, 2)
        to_left = pltpu.roll(now, LANES - 1, 2)
        around = []
        for j in range(tiles):
            for p in range(planes):
                i = j * planes + p
                low = none if j == 0 else to_right[i - planes]
                high = none if j == tiles - 1 else to_left[i + planes]
                left = jnp.where(lane1 == 0, low, to_right[i])
                right = jnp.where(lane1 == LANES - 1, high, to_left[i])
                under = now[i - 1] if p > 0 else none
                over = now[i + 1] if p < planes - 1 else none
                around.append((over + under) + (left + right))
        around = jnp.stack(around) + (after + before)
        source = now + 0.125 * (around - 6.0 * now)
        f = source * m_ref[:, pl.ds(g, BLOCKS, stride=lx), :]
        fx_ref[g] = f
        sum_u = f * qx_ref[g] if g == 0 else sum_u + f * qx_ref[g]
        sum_a = f * px_ref[g] if g == 0 else sum_a + f * px_ref[g]
        before, now = now, after
    sum_u, sum_a = jnp.sum(sum_u, axis=1), jnp.sum(sum_a, axis=1)
    m_first, m_last = 0.125 * m_ref[:, 0, :], 0.125 * m_ref[:, rows - 1, :]
    factor_w = 1.0 - (top_e + top_w)
    factor_a = 1.0 - (top_e + top_a)

    at_row = lax.broadcasted_iota(jnp.int32, (count, LANES), 0)
    at_lane = lax.broadcasted_iota(jnp.int32, (count, LANES), 1)
    on_edge = ((at_row < planes) & (at_lane == 0)) | (
        (at_row >= count - planes) & (at_lane == LANES - 1)
    )

    def spread_edge(value):
        value = jnp.sum(value, axis=1, keepdims=True)
        if count > 2 * planes:
            gap = jnp.zeros((count - 2 * planes, 1), f32)
            value = jnp.concatenate([value[0:planes], gap, value[planes:]], axis=0)
        return jnp.where(on_edge, value, 0.0)

    wait_halos(hr_sem.at[0])
    sides = hyr_ref[...]
    shift_low, shift_high = m_first * hxr_ref[0], m_last * hxr_ref[1]
    rgx[ix, 0] = (sum_u + spread_edge(sides * edge_q)) + (
        top_e * shift_low + factor_w * shift_high
    )
    rgx[ix, 1] = (sum_a + spread_edge(sides * edge_p)) + (
        factor_a * shift_low + top_e * shift_high
    )
    got_rx = exchange(rgx, 2, ix, nx, True)

    for p in range(planes):
        for j in range(tiles):
            mt_ref[p, pl.ds(j * LANES, LANES), :] = m_ref[j * planes + p].T
    joined, nodes_y = sweep_coefficients(mt_ref, ry_ref, ey_ref, turns, ly)
    for c in range(3):
        cgy[iy, c] = joined[c]
    got_cy = exchange(cgy, 1, iy, ny, False)

    spread = jnp.concatenate([sides, jnp.zeros((LANES - 2 * planes, LANES), f32)], axis=0)
    col_ref[...] = spread.T
    u = total = None
    for g in range(lx):
        at = pl.ds(g, BLOCKS, stride=lx)
        column = 0.125 * col_ref[at, :]
        f = fx_ref[g]
        parts = [f[i] for i in range(count)]
        for p in range(planes):
            low = column if p == 0 else pltpu.roll(column, LANES - p, 1)
            high = pltpu.roll(column, LANES - 1 - planes - p, 1)
            i = p
            parts[i] = parts[i] + jnp.where(lane1 == 0, low, 0.0) * m_ref[i, at, :]
            i = (tiles - 1) * planes + p
            parts[i] = parts[i] + jnp.where(lane1 == LANES - 1, high, 0.0) * m_ref[i, at, :]
        f = jnp.stack(parts)
        u = (f if g == 0 else f + u) * rx_ref[g]
        total = u if g == 0 else total + ex_ref[g - 1] * u
        ux_ref[g] = u

    def store_x(g, value):
        vx_ref[g] = value

    own_solution(u, total, nodes_x, count, lx, rx_ref, ex_ref, ux_ref, turns, store_x)

    def store_responses_y(g, e, w):
        at = pl.ds(g, BLOCKS, stride=ly)
        py_ref[:, at, :] = e
        qy_ref[:, at, :] = w

    responses(nodes_y, planes, ly, ry_ref, ey_ref, turns, store_responses_y)
    for p in range(planes):
        for j in range(tiles):
            at = pl.ds(j * LANES, LANES)
            m = mt_ref[p, at, :]
            pm_ref[j * planes + p] = (m * py_ref[p, at, :]).T
            qm_ref[j * planes + p] = (m * qy_ref[p, at, :]).T
    for g in range(lx):
        at = pl.ds(g, BLOCKS, stride=lx)
        pf_ref[g] = pm_ref[:, at, :]
        qf_ref[g] = qm_ref[:, at, :]
    row_of = lax.broadcasted_iota(jnp.int32, (BLOCKS, LANES), 0)
    here = [lax.rem(lane1, lx) == g for g in range(lx)]
    diagonal = lax.div(lane1, lx) == row_of

    def line_sums(step):
        rows_u = rows_a = jnp.zeros((planes, BLOCKS, LANES), f32)
        for g in range(lx):
            v = step(g)
            of_u = jnp.sum((v * qf_ref[g]).reshape(tiles, planes, BLOCKS, LANES), axis=0)
            of_a = jnp.sum((v * pf_ref[g]).reshape(tiles, planes, BLOCKS, LANES), axis=0)
            rows_u = jnp.where(here[g][None], jnp.sum(of_u, axis=2, keepdims=True), rows_u)
            rows_a = jnp.where(here[g][None], jnp.sum(of_a, axis=2, keepdims=True), rows_a)
        return [jnp.sum(jnp.where(diagonal[None], r, 0.0), axis=1) for r in (rows_u, rows_a)]

    own_sums = line_sums(lambda g: vx_ref[g])
    got_cx.wait()
    interface_weights(cgx, ix, nx, sidex, weightx)

    got_rx.wait()
    low, high = outer_values(rgx, weightx, nx)
    low = jnp.broadcast_to((low + shift_low)[:, None, :], shape)
    high = jnp.broadcast_to((high + shift_high)[:, None, :], shape)
    sums = line_sums(lambda g: px_ref[g] * low + qx_ref[g] * high)
    for c in range(2):
        rgy[iy, c] = own_sums[c] + sums[c]
    got_ry = exchange(rgy, 3, iy, ny, False)

    for g in range(lx):
        v = (vx_ref[g] + px_ref[g] * low) + qx_ref[g] * high
        mid_ref[:, pl.ds(g, BLOCKS, stride=lx), :] = v
    for p in range(planes):
        for j in range(tiles):
            midt_ref[p, pl.ds(j * LANES, LANES), :] = mid_ref[j * planes + p].T
    u = total = None
    for g in range(ly):
        at = pl.ds(g, BLOCKS, stride=ly)
        f = midt_ref[:, at, :] * mt_ref[:, at, :]
        u = (f if g == 0 else f + u) * ry_ref[g]
        total = u if g == 0 else total + ey_ref[g - 1] * u
        uy_ref[g] = u

    def store_y(g, value):
        midt_ref[:, pl.ds(g, BLOCKS, stride=ly), :] = value

    own_solution(u, total, nodes_y, planes, ly, ry_ref, ey_ref, uy_ref, turns, store_y)
    got_cy.wait()
    interface_weights(cgy, iy, ny, sidey, weighty)
    wait_halos(hs_sem.at[0])

    got_ry.wait()
    low, high = outer_values(rgy, weighty, ny)
    for p in range(planes):
        for j in range(tiles):
            at = pl.ds(j * LANES, LANES)
            value = midt_ref[p, at, :] + py_ref[p, at, :] * low[p : p + 1]
            value = value + qy_ref[p, at, :] * high[p : p + 1]
            out_ref[p, :, at] = value.T
    pltpu.make_async_copy(sent_ref, sent_ref, ps_sem.at[0]).wait()


def on_device(nx, ny, initial_heat_state, spreading_coefficient):
    planes, rows, columns = initial_heat_state.shape
    count = planes * (columns // LANES)
    lx = rows // BLOCKS
    ly = columns // BLOCKS

    def vmem(*shape):
        return pltpu.VMEM(shape, jnp.float32)

    def dma(number):
        return pltpu.SemaphoreType.DMA((number,))

    natural = vmem(count, rows, LANES)
    turned = vmem(planes, columns, LANES)
    steps_x = vmem(lx, count, BLOCKS, LANES)
    steps_y = vmem(ly, planes, BLOCKS, LANES)
    return pl.pallas_call(
        functools.partial(kernel, nx, ny),
        out_shape=jax.ShapeDtypeStruct((planes, rows, columns), jnp.float32),
        in_specs=[pl.BlockSpec(memory_space=pltpu.HBM)] * 2,
        out_specs=pl.BlockSpec(memory_space=pltpu.VMEM),
        scratch_shapes=[
            natural,
            natural,
            natural,
            turned,
            steps_x,
            steps_x,
            steps_x,
            steps_x,
            steps_x,
            steps_x,
            steps_x,
            natural,
            natural,
            steps_y,
            steps_y,
            steps_y,
            turned,
            turned,
            steps_x,
            steps_x,
            natural,
            turned,
            vmem(count * BLOCKS, LANES),
            vmem(count * BLOCKS, LANES),
            vmem(count * BLOCKS, LANES),
            vmem(count * BLOCKS, LANES),
            vmem(2, count, LANES),
            vmem(2, count, LANES),
            vmem(2 * planes, LANES),
            vmem(2 * planes, LANES),
            vmem(rows, LANES),
            vmem(nx, 3, count, LANES),
            vmem(nx, 2, count, LANES),
            vmem(ny, 3, planes, LANES),
            vmem(ny, 2, planes, LANES),
            vmem(6, nx + 1, count, LANES),
            vmem(6, ny + 1, planes, LANES),
            vmem(nx, 4, count, LANES),
            vmem(ny, 4, planes, LANES),
            dma(2),
            dma(1),
            dma(1),
            dma(1),
            dma(4),
            vmem(5, (nx - 1) * count + (ny - 1) * planes, LANES),
        ],
        compiler_params=pltpu.CompilerParams(
            collective_id=0, has_side_effects=True, vmem_limit_bytes=32 << 20
        ),
    )(
        pltpu.with_memory_space_constraint(initial_heat_state, pltpu.HBM),
        pltpu.with_memory_space_constraint(spreading_coefficient, pltpu.HBM),
    )


def solution(mesh):
    return jax.shard_map(
        functools.partial(on_device, mesh.shape["px"], mesh.shape["py"]),
        mesh=mesh,
        in_specs=(P(None, "px", "py"), P(None, "px", "py")),
        out_specs=P(None, "px", "py"),
        check_vma=False,
    )
```

```python
import functools

import jax
import jax.numpy as jnp
from jax import lax
from jax.experimental import pallas as pl
from jax.experimental.pallas import tpu as pltpu
from jax.sharding import PartitionSpec as P

LANES = 128
BLOCKS = 8
MESH = pl.DeviceIdType.MESH


def combine(left, right):
    e_p, w_p, a_p = left
    e_q, w_q, a_q = right
    gap_p = e_p + w_p
    gap_q = e_q + a_q
    r_p = 1.0 - gap_p
    b_q = 1.0 - gap_q
    inv = 1.0 / (gap_p + r_p * gap_q)
    joined = (
        e_p * e_q * inv,
        w_q + e_q * ((w_p + r_p * a_q) * inv),
        a_p + e_p * ((a_q + b_q * w_p) * inv),
    )
    return joined, (inv, r_p, b_q, e_p, e_q)


def combine_rhs(node, left, right):
    inv, r_p, b_q, e_p, e_q = node
    u_p, a_p = left
    u_q, a_q = right
    p0 = (u_p + r_p * a_q) * inv
    q0 = (a_q + b_q * u_p) * inv
    return (u_q + e_q * p0, a_p + e_p * q0), (p0, q0)


def split(node, start, low, high):
    inv, r_p, b_q, e_p, e_q = node
    p = q = None
    if low is not None:
        from_low = e_p * inv * low
        p, q = from_low, b_q * from_low
    if high is not None:
        from_high = e_q * inv * high
        p = r_p * from_high if p is None else p + r_p * from_high
        q = from_high if q is None else q + from_high
    if start is not None:
        p = start[0] if p is None else start[0] + p
        q = start[1] if q is None else start[1] + q
    return p, q


def tree_coefficients(leaves):
    nodes = []
    while len(leaves) > 1:
        pairs = [combine(leaves[i], leaves[i + 1]) for i in range(0, len(leaves), 2)]
        leaves = [pair[0] for pair in pairs]
        nodes.append([pair[1] for pair in pairs])
    return leaves[0], nodes


def tree_up(nodes, leaves):
    starts = []
    for level in nodes:
        pairs = [
            combine_rhs(level[i], leaves[2 * i], leaves[2 * i + 1]) for i in range(len(level))
        ]
        leaves = [pair[0] for pair in pairs]
        starts.append([pair[1] for pair in pairs])
    return leaves[0], starts


def tree_down(nodes, starts, low, high):
    bounds = [(low, high)]
    for depth in range(len(nodes) - 1, -1, -1):
        below = []
        for i, (lo, hi) in enumerate(bounds):
            start = None if starts is None else starts[depth][i]
            p, q = split(nodes[depth][i], start, lo, hi)
            below += [(lo, q), (p, hi)]
        bounds = below
    zero = jnp.zeros_like(nodes[0][0][0])
    return [tuple(zero if x is None else x for x in pair) for pair in bounds]


def leaf_rows(turn_ref, values, count):
    turn_ref[0 : count * BLOCKS, :] = values.reshape(count * BLOCKS, LANES)
    return [turn_ref[pl.ds(b, count, stride=BLOCKS), :] for b in range(BLOCKS)]


def block_rows(turn_ref, rows, count):
    for b in range(BLOCKS):
        turn_ref[pl.ds(b, count, stride=BLOCKS), :] = rows[b]
    return turn_ref[0 : count * BLOCKS, :].reshape(count, BLOCKS, LANES)


def sweep_coefficients(m_ref, r_ref, e_ref, turn_refs, length):
    count = m_ref.shape[0]
    for g in range(length):
        m = m_ref[:, pl.ds(g, BLOCKS, stride=length), :]
        if g == 0:
            t = 1.0 + m
            r = 1.0 / (1.0 + t)
            e = r
            w = m * r
            a = w
        else:
            t = m + t * r
            r = 1.0 / (1.0 + t)
            w = (m + w) * r
            a = a + e * w
            e = e * r
        r_ref[g] = r
        e_ref[g] = e
    leaves = [leaf_rows(ref, value, count) for ref, value in zip(turn_refs, (e, w, a))]
    return tree_coefficients([tuple(leaf[b] for leaf in leaves) for b in range(BLOCKS)])


def responses(nodes, count, length, r_ref, e_ref, turns, store):
    one = jnp.ones((count, LANES), jnp.float32)
    bounds = tree_down(nodes, None, one, None)
    low_e = block_rows(turns[0], [b[0] for b in bounds], count)
    value_e = block_rows(turns[1], [b[1] for b in bounds], count)
    bounds = tree_down(nodes, None, None, one)
    low_w = block_rows(turns[2], [b[0] for b in bounds], count)
    value_w = block_rows(turns[3], [b[1] for b in bounds], count)
    for g in range(length - 1, -1, -1):
        e, r = e_ref[g], r_ref[g]
        value_e = e * low_e + r * value_e
        value_w = e * low_w + r * value_w
        store(g, value_e, value_w)


def own_solution(u, total, nodes, count, length, r_ref, e_ref, u_ref, turns, store):
    leaves = [leaf_rows(ref, value, count) for ref, value in zip(turns, (u, total))]
    _, starts = tree_up(nodes, list(zip(*leaves)))
    bounds = tree_down(nodes, starts, None, None)
    low = block_rows(turns[0], [b[0] for b in bounds], count)
    value = block_rows(turns[1], [b[1] for b in bounds], count)
    for g in range(length - 1, -1, -1):
        value = (u_ref[g] + e_ref[g] * low) + r_ref[g] * value
        store(g, value)


def interface_weights(gathered, me, n, side_ref, weight_ref):
    blocks = [tuple(gathered[i, c] for c in range(3)) for i in range(n)]
    zero = jnp.zeros_like(blocks[0][0])
    one = jnp.ones_like(zero)
    side_ref[0, 0], side_ref[1, 0] = zero, one
    side_ref[2, n], side_ref[3, n] = zero, one
    total = None
    factor, gap = zero, one
    up = []
    for j in range(n):
        e, w, a = blocks[j]
        t = e / (gap + factor * (e + a))
        up.append((t, factor))
        side_ref[4, j] = t
        total = blocks[j] if total is None else combine(total, blocks[j])[0]
        gap = total[0] + total[1]
        factor = 1.0 - gap
        side_ref[0, j + 1], side_ref[1, j + 1] = factor, gap
    total = None
    factor, gap = zero, one
    down = [None] * n
    for j in range(n - 1, -1, -1):
        e, w, a = blocks[j]
        s = e / ((e + w) + (1.0 - (e + w)) * gap)
        down[j] = (s, factor)
        side_ref[5, j] = s
        total = blocks[j] if total is None else combine(blocks[j], total)[0]
        gap = total[0] + total[2]
        factor = 1.0 - gap
        side_ref[2, j], side_ref[3, j] = factor, gap
    below, above = side_ref[0, me], side_ref[2, me + 1]
    at_low = 1.0 / (side_ref[1, me] + below * side_ref[3, me])
    at_high = 1.0 / (side_ref[1, me + 1] + side_ref[0, me + 1] * side_ref[3, me + 1])
    t, s = side_ref[4, me], side_ref[5, me]
    low_x, low_y = at_low, at_low * below * s
    high_x, high_y = at_high * above * t, at_high
    through = one
    for j in range(n - 1, -1, -1):
        inside = j < me
        keep = jnp.where(inside, through, 0.0)
        t_j, factor_j = up[j]
        other = keep * (t_j * factor_j)
        weight_ref[j, 0], weight_ref[j, 1] = low_x * keep, low_x * other
        weight_ref[j, 2], weight_ref[j, 3] = high_x * keep, high_x * other
        through = jnp.where(inside, through * t_j, through)
    through = one
    for j in range(n):
        inside = j > me
        keep = jnp.where(inside, through, 0.0)
        s_j, factor_j = down[j]
        other = keep * (s_j * factor_j)
        weight_ref[j, 0] += low_y * other
        weight_ref[j, 1] += low_y * keep
        weight_ref[j, 2] += high_y * other
        weight_ref[j, 3] += high_y * keep
        through = jnp.where(inside, through * s_j, through)
    weight_ref[me, 0] = low_y * above
    weight_ref[me, 1] = at_low * below
    weight_ref[me, 2] = at_high * above
    weight_ref[me, 3] = high_x * below


def outer_values(gathered, weight_ref, n):
    low, high = [], []
    for j in range(n):
        u, a = gathered[j, 0], gathered[j, 1]
        low.append(weight_ref[j, 0] * u + weight_ref[j, 1] * a)
        high.append(weight_ref[j, 2] * u + weight_ref[j, 3] * a)
    while len(low) > 1:
        low = [sum(low[i : i + 2]) for i in range(0, len(low), 2)]
        high = [sum(high[i : i + 2]) for i in range(0, len(high), 2)]
    return low[0], high[0]


def partner(me, d, n):
    if n & (n - 1):
        return lax.rem(me + d, n)
    at, b = me, 1
    while b < n:
        if d & b:
            at = at + b - 2 * b * lax.rem(lax.div(me, b), 2)
        b *= 2
    return at


def far_first(n):
    return sorted(range(1, n), key=lambda d: (-(d // 2), d % 2))


def kernel(
    nx,
    ny,
    h_hbm,
    k_hbm,
    out_ref,
    k_ref,
    h_ref,
    m_ref,
    mt_ref,
    rx_ref,
    ex_ref,
    ux_ref,
    fx_ref,
    vx_ref,
    px_ref,
    qx_ref,
    pm_ref,
    qm_ref,
    ry_ref,
    ey_ref,
    uy_ref,
    py_ref,
    qy_ref,
    pf_ref,
    qf_ref,
    mid_ref,
    midt_ref,
    turn0,
    turn1,
    turn2,
    turn3,
    hxs_ref,
    hxr_ref,
    hys_ref,
    hyr_ref,
    col_ref,
    cgx,
    rgx,
    cgy,
    rgy,
    sidex,
    sidey,
    weightx,
    weighty,
    in_sem,
    hs_sem,
    hr_sem,
    ps_sem,
    pr_sem,
    sent_ref,
):
    ix = lax.axis_index("px")
    iy = lax.axis_index("py")
    planes, rows, columns = h_hbm.shape
    tiles = columns // LANES
    count = tiles * planes
    lx = rows // BLOCKS
    ly = columns // BLOCKS
    turns = (turn0, turn1, turn2, turn3)
    f32 = jnp.float32

    def stage(source, target, number):
        for j in range(tiles):
            pltpu.make_async_copy(
                source.at[:, :, pl.ds(j * LANES, LANES)],
                target.at[pl.ds(j * planes, planes)],
                in_sem.at[number],
            ).start()
        return pltpu.make_async_copy(target, target, in_sem.at[number])

    barrier = pltpu.get_barrier_semaphore()
    for d in range(ny - 1, 0, -1):
        pl.semaphore_signal(barrier, inc=1, device_id=(ix, partner(iy, d, ny)), device_id_type=MESH)
    for d in far_first(nx):
        pl.semaphore_signal(barrier, inc=1, device_id=(partner(ix, d, nx), iy), device_id_type=MESH)

    staged_h = stage(h_hbm, h_ref, 0)
    staged_k = stage(k_hbm, k_ref, 1)

    def exchange(ref, number, me, n, along_x):
        def push(to):
            return pltpu.make_async_remote_copy(
                src_ref=ref.at[me],
                dst_ref=ref.at[me],
                send_sem=ps_sem.at[0],
                recv_sem=pr_sem.at[number],
                device_id=(to, iy) if along_x else (ix, to),
                device_id_type=MESH,
            ).start

        pl.when(me > 0)(push(0))
        for d in far_first(n) if along_x else range(n - 1, 0, -1):
            to = partner(me, d, n)
            pl.when(to > 0)(push(to))
        others = ref.at[pl.ds(0, n - 1)]
        return pltpu.make_async_copy(others, others, pr_sem.at[number])

    @pl.when(ix == 0)
    def _():
        hxr_ref[0] = jnp.zeros_like(hxr_ref[0])

    @pl.when(ix == nx - 1)
    def _():
        hxr_ref[1] = jnp.zeros_like(hxr_ref[1])

    low_side = pl.ds(0, planes)
    high_side = pl.ds(planes, planes)

    @pl.when(iy == 0)
    def _():
        hyr_ref[low_side] = jnp.zeros((planes, LANES), f32)

    @pl.when(iy == ny - 1)
    def _():
        hyr_ref[high_side] = jnp.zeros((planes, LANES), f32)

    def halo(source, target, device):
        return pltpu.make_async_remote_copy(
            src_ref=source,
            dst_ref=target,
            send_sem=hs_sem.at[0],
            recv_sem=hr_sem.at[0],
            device_id=device,
            device_id_type=MESH,
        )

    x_down = halo(hxs_ref.at[0], hxr_ref.at[1], (lax.rem(ix + nx - 1, nx), iy))
    x_up = halo(hxs_ref.at[1], hxr_ref.at[0], (lax.rem(ix + 1, nx), iy))
    y_down = halo(
        hys_ref.at[low_side], hyr_ref.at[high_side], (ix, lax.rem(iy + ny - 1, ny))
    )
    y_up = halo(hys_ref.at[high_side], hyr_ref.at[low_side], (ix, lax.rem(iy + 1, ny)))
    routes = (
        (y_up, (iy < ny - 1) & (lax.rem(iy, 2) == 1)),
        (y_down, iy > 0),
        (y_up, (iy < ny - 1) & (lax.rem(iy, 2) == 0)),
        (x_down, ix > 0),
        (x_up, ix < nx - 1),
    )

    def wait_halos(sem):
        inner_x = (ix > 0) & (ix < nx - 1)
        inner_y = (iy > 0) & (iy < ny - 1)
        for two_x in (False, True):
            for two_y in (False, True):
                size = (count * (2 if two_x else 1)) + (planes * (2 if two_y else 1))
                part = turn0.at[pl.ds(0, size)]
                here = (inner_x == two_x) & (inner_y == two_y)
                pl.when(here)(pltpu.make_async_copy(part, part, sem).wait)

    lane = lax.broadcasted_iota(jnp.int32, (rows, LANES), 1)

    def edge_columns(ref):
        packed = jnp.zeros((rows, LANES), f32)
        for p in range(planes):
            low = ref[p]
            high = ref[(tiles - 1) * planes + p]
            packed = jnp.where(lane == p, low if p == 0 else pltpu.roll(low, p, 1), packed)
            packed = jnp.where(lane == planes + p, pltpu.roll(high, planes + p + 1, 1), packed)
        return packed.T[0 : 2 * planes]

    staged_h.wait()
    hxs_ref[0] = h_ref[:, 0, :]
    hxs_ref[1] = h_ref[:, rows - 1, :]
    hys_ref[...] = edge_columns(h_ref)

    pl.semaphore_wait(barrier, nx + ny - 2)
    for copy, sends in routes:
        pl.when(sends)(copy.start)

    staged_k.wait()
    m_ref[...] = 1.0 / k_ref[...]
    joined, nodes_x = sweep_coefficients(m_ref, rx_ref, ex_ref, turns, lx)
    for c in range(3):
        cgx[ix, c] = joined[c]
    got_cx = exchange(cgx, 0, ix, nx, True)
    top_e, top_w, top_a = joined

    def store_responses_x(g, e, w):
        px_ref[g], qx_ref[g] = e, w
        at = pl.ds(g, BLOCKS, stride=lx)
        m = 0.125 * m_ref[:, at, :]
        pm_ref[:, at, :] = m * e
        qm_ref[:, at, :] = m * w

    responses(nodes_x, count, lx, rx_ref, ex_ref, turns, store_responses_x)
    edge_p, edge_q = edge_columns(pm_ref), edge_columns(qm_ref)

    def field(g):
        return h_ref[:, pl.ds(g, BLOCKS, stride=lx), :]

    shape = (count, BLOCKS, LANES)
    sub = lax.broadcasted_iota(jnp.int32, shape, 1)
    lane1 = lax.broadcasted_iota(jnp.int32, (BLOCKS, LANES), 1)
    none = jnp.zeros((BLOCKS, LANES), f32)
    now = field(0)
    before = jnp.where(sub == 0, 0.0, pltpu.roll(field(lx - 1), 1, 1))
    beyond = jnp.where(sub == BLOCKS - 1, 0.0, pltpu.roll(now, BLOCKS - 1, 1))
    sum_u = sum_a = None
    for g in range(lx):
        after = field(g + 1) if g + 1 < lx else beyond
        to_right = pltpu.roll(now, 1, 2)
        to_left = pltpu.roll(now, LANES - 1, 2)
        around = []
        for j in range(tiles):
            for p in range(planes):
                i = j * planes + p
                low = none if j == 0 else to_right[i - planes]
                high = none if j == tiles - 1 else to_left[i + planes]
                left = jnp.where(lane1 == 0, low, to_right[i])
                right = jnp.where(lane1 == LANES - 1, high, to_left[i])
                under = now[i - 1] if p > 0 else none
                over = now[i + 1] if p < planes - 1 else none
                around.append((over + under) + (left + right))
        around = jnp.stack(around) + (after + before)
        source = now + 0.125 * (around - 6.0 * now)
        f = source * m_ref[:, pl.ds(g, BLOCKS, stride=lx), :]
        fx_ref[g] = f
        sum_u = f * qx_ref[g] if g == 0 else sum_u + f * qx_ref[g]
        sum_a = f * px_ref[g] if g == 0 else sum_a + f * px_ref[g]
        before, now = now, after
    sum_u, sum_a = jnp.sum(sum_u, axis=1), jnp.sum(sum_a, axis=1)
    m_first, m_last = 0.125 * m_ref[:, 0, :], 0.125 * m_ref[:, rows - 1, :]
    factor_w = 1.0 - (top_e + top_w)
    factor_a = 1.0 - (top_e + top_a)

    at_row = lax.broadcasted_iota(jnp.int32, (count, LANES), 0)
    at_lane = lax.broadcasted_iota(jnp.int32, (count, LANES), 1)
    on_edge = ((at_row < planes) & (at_lane == 0)) | (
        (at_row >= count - planes) & (at_lane == LANES - 1)
    )

    def spread_edge(value):
        value = jnp.sum(value, axis=1, keepdims=True)
        if count > 2 * planes:
            gap = jnp.zeros((count - 2 * planes, 1), f32)
            value = jnp.concatenate([value[0:planes], gap, value[planes:]], axis=0)
        return jnp.where(on_edge, value, 0.0)

    wait_halos(hr_sem.at[0])
    sides = hyr_ref[...]
    shift_low, shift_high = m_first * hxr_ref[0], m_last * hxr_ref[1]
    rgx[ix, 0] = (sum_u + spread_edge(sides * edge_q)) + (
        top_e * shift_low + factor_w * shift_high
    )
    rgx[ix, 1] = (sum_a + spread_edge(sides * edge_p)) + (
        factor_a * shift_low + top_e * shift_high
    )
    got_rx = exchange(rgx, 2, ix, nx, True)

    for p in range(planes):
        for j in range(tiles):
            mt_ref[p, pl.ds(j * LANES, LANES), :] = m_ref[j * planes + p].T
    joined, nodes_y = sweep_coefficients(mt_ref, ry_ref, ey_ref, turns, ly)
    for c in range(3):
        cgy[iy, c] = joined[c]
    got_cy = exchange(cgy, 1, iy, ny, False)

    spread = jnp.concatenate([sides, jnp.zeros((LANES - 2 * planes, LANES), f32)], axis=0)
    col_ref[...] = spread.T
    u = total = None
    for g in range(lx):
        at = pl.ds(g, BLOCKS, stride=lx)
        column = 0.125 * col_ref[at, :]
        f = fx_ref[g]
        parts = [f[i] for i in range(count)]
        for p in range(planes):
            low = column if p == 0 else pltpu.roll(column, LANES - p, 1)
            high = pltpu.roll(column, LANES - 1 - planes - p, 1)
            i = p
            parts[i] = parts[i] + jnp.where(lane1 == 0, low, 0.0) * m_ref[i, at, :]
            i = (tiles - 1) * planes + p
            parts[i] = parts[i] + jnp.where(lane1 == LANES - 1, high, 0.0) * m_ref[i, at, :]
        f = jnp.stack(parts)
        u = (f if g == 0 else f + u) * rx_ref[g]
        total = u if g == 0 else total + ex_ref[g - 1] * u
        ux_ref[g] = u

    def store_x(g, value):
        vx_ref[g] = value

    own_solution(u, total, nodes_x, count, lx, rx_ref, ex_ref, ux_ref, turns, store_x)

    def store_responses_y(g, e, w):
        at = pl.ds(g, BLOCKS, stride=ly)
        py_ref[:, at, :] = e
        qy_ref[:, at, :] = w

    responses(nodes_y, planes, ly, ry_ref, ey_ref, turns, store_responses_y)
    for p in range(planes):
        for j in range(tiles):
            at = pl.ds(j * LANES, LANES)
            m = mt_ref[p, at, :]
            pm_ref[j * planes + p] = (m * py_ref[p, at, :]).T
            qm_ref[j * planes + p] = (m * qy_ref[p, at, :]).T
    for g in range(lx):
        at = pl.ds(g, BLOCKS, stride=lx)
        pf_ref[g] = pm_ref[:, at, :]
        qf_ref[g] = qm_ref[:, at, :]
    row_of = lax.broadcasted_iota(jnp.int32, (BLOCKS, LANES), 0)
    here = [lax.rem(lane1, lx) == g for g in range(lx)]
    diagonal = lax.div(lane1, lx) == row_of

    def line_sums(step):
        rows_u = rows_a = jnp.zeros((planes, BLOCKS, LANES), f32)
        for g in range(lx):
            v = step(g)
            of_u = jnp.sum((v * qf_ref[g]).reshape(tiles, planes, BLOCKS, LANES), axis=0)
            of_a = jnp.sum((v * pf_ref[g]).reshape(tiles, planes, BLOCKS, LANES), axis=0)
            rows_u = jnp.where(here[g][None], jnp.sum(of_u, axis=2, keepdims=True), rows_u)
            rows_a = jnp.where(here[g][None], jnp.sum(of_a, axis=2, keepdims=True), rows_a)
        return [jnp.sum(jnp.where(diagonal[None], r, 0.0), axis=1) for r in (rows_u, rows_a)]

    own_sums = line_sums(lambda g: vx_ref[g])
    got_cx.wait()
    interface_weights(cgx, ix, nx, sidex, weightx)

    got_rx.wait()
    low, high = outer_values(rgx, weightx, nx)
    low = jnp.broadcast_to((low + shift_low)[:, None, :], shape)
    high = jnp.broadcast_to((high + shift_high)[:, None, :], shape)
    sums = line_sums(lambda g: px_ref[g] * low + qx_ref[g] * high)
    for c in range(2):
        rgy[iy, c] = own_sums[c] + sums[c]
    got_ry = exchange(rgy, 3, iy, ny, False)

    for g in range(lx):
        v = (vx_ref[g] + px_ref[g] * low) + qx_ref[g] * high
        mid_ref[:, pl.ds(g, BLOCKS, stride=lx), :] = v
    for p in range(planes):
        for j in range(tiles):
            midt_ref[p, pl.ds(j * LANES, LANES), :] = mid_ref[j * planes + p].T
    u = total = None
    for g in range(ly):
        at = pl.ds(g, BLOCKS, stride=ly)
        f = midt_ref[:, at, :] * mt_ref[:, at, :]
        u = (f if g == 0 else f + u) * ry_ref[g]
        total = u if g == 0 else total + ey_ref[g - 1] * u
        uy_ref[g] = u

    def store_y(g, value):
        midt_ref[:, pl.ds(g, BLOCKS, stride=ly), :] = value

    own_solution(u, total, nodes_y, planes, ly, ry_ref, ey_ref, uy_ref, turns, store_y)
    kept = planes // 2
    for p in range(kept, planes):
        for j in range(tiles):
            at = pl.ds(j * LANES, LANES)
            mid_ref[j * planes + p] = midt_ref[p, at, :].T
            pm_ref[j * planes + p] = py_ref[p, at, :].T
            qm_ref[j * planes + p] = qy_ref[p, at, :].T
    got_cy.wait()
    interface_weights(cgy, iy, ny, sidey, weighty)
    wait_halos(hs_sem.at[0])

    got_ry.wait()
    low, high = outer_values(rgy, weighty, ny)
    spread = jnp.concatenate([low, high, jnp.zeros((LANES - 2 * planes, LANES), f32)], axis=0)
    turned = spread.T
    for p in range(kept):
        for j in range(tiles):
            at = pl.ds(j * LANES, LANES)
            value = midt_ref[p, at, :] + py_ref[p, at, :] * low[p : p + 1]
            value = value + qy_ref[p, at, :] * high[p : p + 1]
            out_ref[p, :, at] = value.T
    for p in range(kept, planes):
        low, high = turned[:, p : p + 1], turned[:, planes + p : planes + p + 1]
        for j in range(tiles):
            i = j * planes + p
            value = (mid_ref[i] + pm_ref[i] * low) + qm_ref[i] * high
            out_ref[p, :, pl.ds(j * LANES, LANES)] = value
    pltpu.make_async_copy(sent_ref, sent_ref, ps_sem.at[0]).wait()


def on_device(nx, ny, initial_heat_state, spreading_coefficient):
    planes, rows, columns = initial_heat_state.shape
    count = planes * (columns // LANES)
    lx = rows // BLOCKS
    ly = columns // BLOCKS

    def vmem(*shape):
        return pltpu.VMEM(shape, jnp.float32)

    def dma(number):
        return pltpu.SemaphoreType.DMA((number,))

    natural = vmem(count, rows, LANES)
    turned = vmem(planes, columns, LANES)
    steps_x = vmem(lx, count, BLOCKS, LANES)
    steps_y = vmem(ly, planes, BLOCKS, LANES)
    return pl.pallas_call(
        functools.partial(kernel, nx, ny),
        out_shape=jax.ShapeDtypeStruct((planes, rows, columns), jnp.float32),
        in_specs=[pl.BlockSpec(memory_space=pltpu.HBM)] * 2,
        out_specs=pl.BlockSpec(memory_space=pltpu.VMEM),
        scratch_shapes=[
            natural,
            natural,
            natural,
            turned,
            steps_x,
            steps_x,
            steps_x,
            steps_x,
            steps_x,
            steps_x,
            steps_x,
            natural,
            natural,
            steps_y,
            steps_y,
            steps_y,
            turned,
            turned,
            steps_x,
            steps_x,
            natural,
            turned,
            vmem(count * BLOCKS, LANES),
            vmem(count * BLOCKS, LANES),
            vmem(count * BLOCKS, LANES),
            vmem(count * BLOCKS, LANES),
            vmem(2, count, LANES),
            vmem(2, count, LANES),
            vmem(2 * planes, LANES),
            vmem(2 * planes, LANES),
            vmem(rows, LANES),
            vmem(nx, 3, count, LANES),
            vmem(nx, 2, count, LANES),
            vmem(ny, 3, planes, LANES),
            vmem(ny, 2, planes, LANES),
            vmem(6, nx + 1, count, LANES),
            vmem(6, ny + 1, planes, LANES),
            vmem(nx, 4, count, LANES),
            vmem(ny, 4, planes, LANES),
            dma(2),
            dma(1),
            dma(1),
            dma(1),
            dma(4),
            vmem(5, (nx - 1) * count + (ny - 1) * planes, LANES),
        ],
        compiler_params=pltpu.CompilerParams(
            collective_id=0, has_side_effects=True, vmem_limit_bytes=32 << 20
        ),
    )(
        pltpu.with_memory_space_constraint(initial_heat_state, pltpu.HBM),
        pltpu.with_memory_space_constraint(spreading_coefficient, pltpu.HBM),
    )


def solution(mesh):
    return jax.shard_map(
        functools.partial(on_device, mesh.shape["px"], mesh.shape["py"]),
        mesh=mesh,
        in_specs=(P(None, "px", "py"), P(None, "px", "py")),
        out_specs=P(None, "px", "py"),
        check_vma=False,
    )
```
